32 devices in a mesh: subj: 2 (over x), row: 8 (over z, y), col: 2 (over core).
Axes of the slice: x: 2, y: 2, z: 4, core: 2. Of those that a mesh axis runs over, the one named last changes fastest.
Arguments:
- series: float32 [256, 11392], P(('subj', 'row', 'col')), parts along dimension 0, may hold values from -30 to 30
- tap_values: float32 [17], replicated, may hold values from -4 to 4
- tap_count: int32 [1], replicated, may hold values from 4 to 8
- kept_frames: int32 [32], P('subj'), parts along dimension 0, may hold values from 1 to 8, 96 in all
- band_start: int32 [2], P('subj'), parts along dimension 0, may hold values from 0 to 7296
Outputs:
- fisher_band: bfloat16 [8192, 11392], P('subj', ('row', 'col')), parts along dimension 0
The draws below stay inside these ranges and needn't reach their ends.
There are 2 independent parts, one for each index of `subj`. The reference program is written for one: setup_inputs(seed, part) draws one part's arguments, and reference() takes and returns one part's arrays. A program takes and returns all parts, laid end to end along the dimension named above; an argument that names none is the same for every part. Nothing has to cross between parts.
Inputs may be any that keep to these rules, and one draw needn't show every extreme that they name: `tap_count`: frames farther than this from the centre get no weight. Time block d holds frames d * 8 to (d + 1) * 8 - 1; only its first kept_frames[d] frames are kept. `band_start`: the 4096 band grayordinates lie inside the grid.
All inputs are finite; a program needn't handle non-finite values.
Results may differ from the reference program's by a relative error of at most 0.0031.
The reference program's roundings to bfloat16 on the way (of `scaled`) count: a program that leaves them out, or rounds other values in their place, can miss the bound.
Values may be sent and summed in bfloat16 or wider, within the bound.
No kernel may reach another device: no remote copies, remote signals or barrier semaphores. Data moves between devices by JAX's collectives and lax.ppermute only.
A program may use at most 128 MiB of HBM per device.

```python
import math
import jax
import jax.numpy as jnp
import numpy as np
from jax import lax

FR_DEV = 8
B = 4096
KMAX = 8
FRAMES = 128
G = 11392
N_ROW = 8
N_COL = 2


def draw_series(key, part):
    subkeys = jax.random.split(key, 4)
    network = jax.random.randint(subkeys[0], (G,), 0, 16)
    courses = jax.random.truncated_normal(subkeys[1], -4.0, 4.0, (FRAMES, 16), jnp.float32)
    loadings = jax.random.uniform(subkeys[2], (G,), jnp.float32, 0.5, 1.5)
    noise_part = jax.random.truncated_normal(subkeys[3], -4.0, 4.0, (FRAMES, G), jnp.float32)
    drift_scale = 3.0 - 2.0 * jnp.arange(FRAMES, dtype=jnp.float32) / FRAMES
    signal = jnp.take(courses, network, axis=1) * loadings
    return (signal + noise_part) * drift_scale[:, None]


def split_up(count, total, bound, slope):
    weights = [(1 << 20) // math.isqrt(rank ** slope) + 1 for rank in range(2, count + 1)]
    rest, holding = total - bound - (count - 1), [1] * (count - 1)
    while rest > 0:
        candidates = [i for i in range(count - 1) if holding[i] < bound]
        pool, budget = sum([weights[i] for i in candidates]), rest
        for i in candidates:
            extra = min(bound - holding[i], max(1, budget * weights[i] // pool), rest)
            holding[i] = holding[i] + extra
            rest = rest - extra
    return np.array([bound] + holding)


def uneven(stream_key, amount, total, limit, lean):
    if amount == 2:
        one = jax.random.randint(stream_key, (), max(1, total - limit), min(limit, total - 1) + 1)
        return jnp.stack([one, total - one])
    sizes = jnp.asarray(split_up(amount, total, limit, lean), jnp.int32)
    couples = (amount - 1) // 2
    giver, sink = sizes[1:1 + 2 * couples:2], sizes[2:2 + 2 * couples:2]
    slack = jnp.minimum(giver - 1, limit - sink)
    shifted = jax.random.randint(jax.random.fold_in(stream_key, 1), (couples,), 0, 1 << 20) % (slack + 1)
    sizes = sizes.at[1:1 + 2 * couples:2].set(giver - shifted).at[2:2 + 2 * couples:2].set(sink + shifted)
    return sizes[jax.random.permutation(jax.random.fold_in(stream_key, 2), amount)]


def bell_draw(rng, dims, deviation, bound, kind=jnp.bfloat16):
    values = deviation * jax.random.normal(rng, dims, jnp.float32)
    return jnp.clip(values, min=-bound, max=bound).astype(kind)


def setup_inputs(seed: int = 0, part: int = 0) -> dict:
    key_list = jax.random.split(jax.random.key(seed), 6)
    own_keys = jax.random.split(jax.random.fold_in(key_list[5], part), 6)
    return {
        "series": draw_series(jax.random.fold_in(jax.random.fold_in(key_list[5], part), 71), part),
        "tap_values": bell_draw(key_list[1], (2 * KMAX + 1,), 1.0, 4.0, jnp.float32),
        "tap_count": jax.random.randint(key_list[2], (1,), KMAX // 2, KMAX + 1).astype(jnp.int32),
        "kept_frames": uneven(own_keys[3], N_ROW * N_COL, 3 * FRAMES // 4, FR_DEV, 0).astype(jnp.int32),
        "band_start": jax.random.randint(own_keys[4], (1,), 0, G - B + 1).astype(jnp.int32),
    }


EPSILON = 1e-06
CLIP_LIMIT = 0.999

def tap_table(tap_values, tap_count):
    tap_reach = tap_values.shape[0] // 2
    offsets = jnp.arange(tap_values.shape[0], dtype=jnp.int32) - tap_reach
    active = (jnp.abs(offsets) <= tap_count[0]).astype(jnp.float32)
    centre = jnp.sum(active * tap_values) / jnp.sum(active)
    return active * (tap_values - centre)

def band_filter(padded, tap_weights, length):
    filtered = tap_weights[0] * padded[0:length]
    for tap_index in range(1, tap_weights.shape[0]):
        filtered = filtered + tap_weights[tap_index] * padded[tap_index:tap_index + length]
    return filtered

def keep_table(kept_frames, frames, block_len):
    positions = jnp.arange(frames, dtype=jnp.int32)
    return (positions % block_len < kept_frames[positions // block_len]).astype(jnp.float32)[:, None]

def normalize(filtered, keep_mask):
    centered = keep_mask * filtered
    spread = lax.optimization_barrier(jnp.sum(centered * centered, axis=0))
    return (centered * lax.rsqrt(spread + EPSILON)).astype(jnp.bfloat16)

def fisher_z(correlation):
    clipped = jnp.clip(correlation, -CLIP_LIMIT, CLIP_LIMIT)
    return 0.5 * (jnp.log1p(clipped) - jnp.log1p(-clipped))

def reference(series, tap_values, tap_count, kept_frames, band_start):
    tap_weights = tap_table(tap_values, tap_count)
    padded = jnp.pad(series, ((KMAX, KMAX), (0, 0)))
    filtered = band_filter(padded, tap_weights, FRAMES)
    keep_mask = keep_table(kept_frames, FRAMES, FR_DEV)
    scaled = normalize(filtered, keep_mask)
    band_cols = lax.dynamic_slice_in_dim(scaled, band_start[0], B, 1)
    correlation = lax.dot_general(band_cols, scaled, (((0,), (0,)), ((), ())), preferred_element_type=jnp.float32)
    return fisher_z(correlation).astype(jnp.bfloat16)
```

```python
import functools

import jax
import jax.numpy as jnp
from jax import lax
from jax.experimental import pallas as pl
from jax.experimental.pallas import tpu as pltpu
from jax.sharding import PartitionSpec as P

B = 4096
LANES = 128
EPSILON = 1e-06
CLIP_LIMIT = 0.999
AXES = ("row", "col")


def round_up(value, unit):
    return (value + unit - 1) // unit * unit


def band_place(device, n_row):
    row, col = device // 2, device % 2
    return (col * 2 + row % 2) * (n_row // 2) + row // 2


def pack_kernel(n_row, own, own_pad, share, start_ref, series_ref, out_ref, band_ref):
    n_dev = 2 * n_row
    total = series_ref.shape[1]
    start = start_ref[0]
    base = pl.multiple_of(jnp.minimum(start // LANES * LANES, total - B - LANES), LANES)
    rest = start - base
    shift = lax.rem(LANES - rest, LANES)
    lane = lax.broadcasted_iota(jnp.int32, (8, LANES), 1)
    here = lane < LANES - rest
    before = pltpu.roll(series_ref[:, pl.ds(base, LANES)], shift, 1)
    for tile in range(B // LANES):
        after = pltpu.roll(series_ref[:, pl.ds(base + (tile + 1) * LANES, LANES)], shift, 1)
        band_ref[:, tile * LANES : (tile + 1) * LANES] = jnp.where(here, before, after)
        before = after
    for device in range(n_dev):
        place = band_place(device, n_row)
        out_ref[device, :, :own] = series_ref[:, device * own : (device + 1) * own]
        if own_pad > own:
            out_ref[device, :, own:own_pad] = jnp.zeros((8, own_pad - own), jnp.float32)
        out_ref[device, :, own_pad : own_pad + share] = band_ref[:, place * share : (place + 1) * share]


def filter_matrix(kept, frames, taps_ref, count_ref, kept_ref):
    n_taps = taps_ref.shape[0]
    reach = n_taps // 2
    shape = (kept, LANES)
    place = lax.broadcasted_iota(jnp.int32, shape, 0)

    def skip(block, carry):
        frame, seen = carry
        seen = seen + kept_ref[block]
        return frame + jnp.where(place >= seen, 8 - kept_ref[block], 0), seen

    frame, _ = lax.fori_loop(0, frames // 8, skip, (place, jnp.int32(0)), unroll=frames <= 128)
    reach_used = count_ref[0]
    tap_sum = jnp.float32(0)
    tap_number = jnp.float32(0)
    for tap in range(n_taps):
        used = abs(tap - reach) <= reach_used
        tap_sum = tap_sum + jnp.where(used, taps_ref[tap], 0.0)
        tap_number = tap_number + jnp.where(used, 1.0, 0.0)
    centre = jnp.full(shape, tap_sum, jnp.float32) / jnp.full(shape, tap_number, jnp.float32)
    pieces = []
    for tile in range(frames // LANES):
        offset = lax.broadcasted_iota(jnp.int32, shape, 1) + tile * LANES - frame
        value = jnp.zeros(shape, jnp.float32)
        for tap in range(n_taps):
            value = jnp.where(offset == tap - reach, taps_ref[tap], value)
        pieces.append(jnp.where(jnp.abs(offset) <= reach_used, value - centre, 0.0))
    return pieces[0] if len(pieces) == 1 else jnp.concatenate(pieces, 1)


def scale_kernel(own, own_pad, taps_ref, count_ref, kept_ref, raw_ref, own_ref, band_ref):
    kept = band_ref.shape[0]
    frames = raw_ref.shape[0]
    matrix = filter_matrix(kept, frames, taps_ref, count_ref, kept_ref)
    centered = jnp.dot(
        matrix, raw_ref[...], precision=lax.Precision.HIGHEST, preferred_element_type=jnp.float32
    )
    spread = jnp.sum(centered * centered, axis=0, keepdims=True)
    scaled = centered * lax.rsqrt(spread + EPSILON)
    own_ref[...] = scaled[:, :own_pad].T[:own].astype(jnp.bfloat16)
    band_ref[...] = scaled[:, own_pad : own_pad + band_ref.shape[1]].astype(jnp.bfloat16)


def fisher_kernel(place_ref, own_ref, a_ref, b_ref, c_ref, d_ref, out_ref):
    share = a_ref.shape[2]
    z = place_ref[0]
    for k, ref in enumerate((a_ref, b_ref, c_ref, d_ref)):
        @pl.when(pl.program_id(0) == k)
        def _(ref=ref):
            for step in range(ref.shape[0]):
                correlation = jnp.dot(
                    own_ref[...], ref[step], preferred_element_type=jnp.float32
                )
                clipped = jnp.clip(correlation, -CLIP_LIMIT, CLIP_LIMIT)
                z_value = 0.5 * (jnp.log(1.0 + clipped) - jnp.log(1.0 - clipped))
                where = pl.multiple_of((z ^ step) * share, share)
                out_ref[:, pl.ds(where, share)] = z_value.astype(jnp.bfloat16)


def body(series, tap_values, tap_count, kept_frames, band_start):
    n_row = lax.axis_size("row")
    n_dev = n_row * lax.axis_size("col")
    frames = 8 * n_dev
    kept = frames * 3 // 4
    own = series.shape[1] // n_dev
    own_pad = round_up(own, LANES)
    share = B // n_dev
    width = own_pad + round_up(share, LANES)
    n_quarter = n_row // 2
    smem = pl.BlockSpec(memory_space=pltpu.SMEM)
    vmem = pl.BlockSpec(memory_space=pltpu.VMEM)

    packed = pl.pallas_call(
        functools.partial(pack_kernel, n_row, own, own_pad, share),
        out_shape=jax.ShapeDtypeStruct((n_dev, 8, width), jnp.float32),
        in_specs=[smem, vmem],
        out_specs=vmem,
        scratch_shapes=[pltpu.VMEM((8, B), jnp.float32)],
        compiler_params=pltpu.CompilerParams(vmem_limit_bytes=48 << 20),
    )(band_start, series)
    raw = lax.all_to_all(packed, AXES, 0, 0, tiled=True).reshape(frames, width)
    own_rows, block = pl.pallas_call(
        functools.partial(scale_kernel, own, own_pad),
        out_shape=(
            jax.ShapeDtypeStruct((own, kept), jnp.bfloat16),
            jax.ShapeDtypeStruct((kept, share), jnp.bfloat16),
        ),
        in_specs=[smem, smem, smem, vmem],
        out_specs=(vmem, vmem),
        compiler_params=pltpu.CompilerParams(vmem_limit_bytes=48 << 20),
    )(tap_values, tap_count, kept_frames, raw)

    def swap_row(x, bits):
        return lax.ppermute(x, "row", [(i, i ^ bits) for i in range(n_row)])

    def swap_col(x):
        return lax.ppermute(x, "col", [(0, 1), (1, 0)])

    row, col = lax.axis_index("row"), lax.axis_index("col")
    first = row // 2
    line = jnp.stack([block] + [swap_row(block, 2 * step) for step in range(1, n_quarter)])
    if share % LANES:
        line = jnp.take(line, jnp.arange(n_quarter, dtype=jnp.int32) ^ first, axis=0)
        line = line.transpose(1, 0, 2).reshape(1, kept, n_quarter * share)
        first = jnp.zeros_like(first)
    line_y = swap_row(line, 1)
    line_c = swap_col(line)
    line_yc = swap_col(line_y)

    place = jnp.stack([first, col * 2 + row % 2]).astype(jnp.int32)
    out = pl.pallas_call(
        fisher_kernel,
        out_shape=jax.ShapeDtypeStruct((own, B), jnp.bfloat16),
        grid_spec=pltpu.PrefetchScalarGridSpec(
            num_scalar_prefetch=1,
            grid=(4,),
            in_specs=[vmem] * 5,
            out_specs=pl.BlockSpec((own, B // 4), lambda k, p: (0, p[1] ^ k)),
        ),
        compiler_params=pltpu.CompilerParams(vmem_limit_bytes=48 << 20),
    )(place, own_rows, line, line_y, line_c, line_yc)
    return out.T


def solution(mesh):
    placed = (P(("subj", "row", "col"), None), P(), P(), P("subj"), P("subj"))
    return jax.shard_map(
        body, mesh=mesh, in_specs=placed, out_specs=P("subj", ("row", "col")), check_vma=False
    )
```

```python
import functools

import jax
import jax.numpy as jnp
from jax import lax
from jax.experimental import pallas as pl
from jax.experimental.pallas import tpu as pltpu
from jax.sharding import PartitionSpec as P

B = 4096
LANES = 128
EPSILON = 1e-06
CLIP_LIMIT = 0.999
AXES = ("row", "col")


def round_up(value, unit):
    return (value + unit - 1) // unit * unit


def band_place(device, n_row):
    row, col = device // 2, device % 2
    return (col * 2 + row % 2) * (n_row // 2) + row // 2


def pack_band_kernel(n_row, share, start_ref, series_ref, out_ref, window_ref, band_ref, sem):
    total = series_ref.shape[1]
    start = start_ref[0]
    base = pl.multiple_of(jnp.minimum(start // LANES * LANES, total - B - LANES), LANES)
    rest = start - base
    shift = lax.rem(LANES - rest, LANES)
    load = pltpu.make_async_copy(series_ref.at[:, pl.ds(base, B + LANES)], window_ref, sem)
    load.start()
    lane = lax.broadcasted_iota(jnp.int32, (8, LANES), 1)
    here = lane < LANES - rest
    load.wait()
    before = pltpu.roll(window_ref[:, :LANES], shift, 1)
    for tile in range(B // LANES):
        after = pltpu.roll(window_ref[:, (tile + 1) * LANES : (tile + 2) * LANES], shift, 1)
        band_ref[:, tile * LANES : (tile + 1) * LANES] = jnp.where(here, before, after)
        before = after
    for device in range(2 * n_row):
        place = band_place(device, n_row)
        out_ref[device, :, :share] = band_ref[:, place * share : (place + 1) * share]


def pack_own_kernel(own, taps_ref, count_ref, kept_ref, series_ref, out_ref, matrix_ref):
    kept, frames = matrix_ref.shape
    matrix_ref[...] = filter_matrix(kept, frames, taps_ref, count_ref, kept_ref)
    own_pad = out_ref.shape[2]
    for device in range(out_ref.shape[0]):
        out_ref[device, :, :own] = series_ref[:, device * own : (device + 1) * own]
        if own_pad > own:
            out_ref[device, :, own:] = jnp.zeros((8, own_pad - own), jnp.float32)


def filter_matrix(kept, frames, taps_ref, count_ref, kept_ref):
    n_taps = taps_ref.shape[0]
    reach = n_taps // 2
    shape = (kept, LANES)
    place = lax.broadcasted_iota(jnp.int32, shape, 0)

    def skip(block, carry):
        frame, seen = carry
        seen = seen + kept_ref[block]
        return frame + jnp.where(place >= seen, 8 - kept_ref[block], 0), seen

    frame, _ = lax.fori_loop(0, frames // 8, skip, (place, jnp.int32(0)), unroll=frames <= 128)
    reach_used = count_ref[0]
    tap_sum = jnp.float32(0)
    tap_number = jnp.float32(0)
    for tap in range(n_taps):
        used = abs(tap - reach) <= reach_used
        tap_sum = tap_sum + jnp.where(used, taps_ref[tap], 0.0)
        tap_number = tap_number + jnp.where(used, 1.0, 0.0)
    centre = jnp.full(shape, tap_sum, jnp.float32) / jnp.full(shape, tap_number, jnp.float32)
    pieces = []
    for tile in range(frames // LANES):
        offset = lax.broadcasted_iota(jnp.int32, shape, 1) + tile * LANES - frame
        value = jnp.zeros(shape, jnp.float32)
        for tap in range(n_taps):
            value = jnp.where(offset == tap - reach, taps_ref[tap], value)
        pieces.append(jnp.where(jnp.abs(offset) <= reach_used, value - centre, 0.0))
    return pieces[0] if len(pieces) == 1 else jnp.concatenate(pieces, 1)


def scaled_columns(matrix_ref, raw_ref):
    centered = jnp.dot(
        matrix_ref[...],
        raw_ref[...],
        precision=lax.Precision.HIGHEST,
        preferred_element_type=jnp.float32,
    )
    spread = jnp.sum(centered * centered, axis=0, keepdims=True)
    return centered * lax.rsqrt(spread + EPSILON)


def scale_band_kernel(matrix_ref, raw_ref, band_ref):
    scaled = scaled_columns(matrix_ref, raw_ref)
    band_ref[...] = scaled[:, : band_ref.shape[1]].astype(jnp.bfloat16)


def scale_own_kernel(matrix_ref, raw_ref, own_ref):
    scaled = scaled_columns(matrix_ref, raw_ref)
    own_ref[...] = scaled.T[: own_ref.shape[0]].astype(jnp.bfloat16)


def fisher_kernel(place_ref, own_ref, line_ref, *refs):
    out_ref = refs[-1]
    blocks, _, width = line_ref.shape
    z = place_ref[0] % blocks
    for step in range(blocks):
        correlation = jnp.dot(own_ref[...], line_ref[step], preferred_element_type=jnp.float32)
        clipped = jnp.clip(correlation, -CLIP_LIMIT, CLIP_LIMIT)
        z_value = 0.5 * (jnp.log(1.0 + clipped) - jnp.log(1.0 - clipped))
        where = pl.multiple_of((z ^ step) * width, width)
        out_ref[:, pl.ds(where, width)] = z_value.astype(jnp.bfloat16)


def fisher_quarter(place, own_rows, line, out, k):
    blocks, kept, width = line.shape
    parts = 2 if blocks % 2 == 0 else 1
    step_blocks = blocks // parts
    own = own_rows.shape[0]
    specs = [
        pl.BlockSpec((own, kept), lambda j, p: (0, 0)),
        pl.BlockSpec((step_blocks, kept, width), lambda j, p: (j, 0, 0)),
    ]
    args = [place, own_rows, line]
    aliases = {}
    if out is not None:
        specs.append(pl.BlockSpec(memory_space=pl.ANY))
        args.append(out)
        aliases = {3: 0}
    return pl.pallas_call(
        fisher_kernel,
        out_shape=jax.ShapeDtypeStruct((own, B), jnp.bfloat16),
        grid_spec=pltpu.PrefetchScalarGridSpec(
            num_scalar_prefetch=1,
            grid=(parts,),
            in_specs=specs,
            out_specs=pl.BlockSpec(
                (own, B // 4 // parts),
                lambda j, p: (0, (p[1] ^ k) * parts + ((p[0] // step_blocks) ^ j)),
            ),
        ),
        input_output_aliases=aliases,
        compiler_params=pltpu.CompilerParams(vmem_limit_bytes=48 << 20),
    )(*args)


def body(series, tap_values, tap_count, kept_frames, band_start):
    n_row = lax.axis_size("row")
    n_dev = n_row * lax.axis_size("col")
    frames = 8 * n_dev
    kept = frames * 3 // 4
    own = series.shape[1] // n_dev
    own_pad = round_up(own, LANES)
    share = B // n_dev
    share_pad = round_up(share, LANES)
    n_quarter = n_row // 2
    smem = pl.BlockSpec(memory_space=pltpu.SMEM)
    vmem = pl.BlockSpec(memory_space=pltpu.VMEM)
    params = pltpu.CompilerParams(vmem_limit_bytes=48 << 20)

    packed_band = pl.pallas_call(
        functools.partial(pack_band_kernel, n_row, share),
        out_shape=jax.ShapeDtypeStruct((n_dev, 8, share_pad), jnp.float32),
        in_specs=[smem, pl.BlockSpec(memory_space=pltpu.HBM)],
        out_specs=vmem,
        scratch_shapes=[
            pltpu.VMEM((8, B + LANES), jnp.float32),
            pltpu.VMEM((8, B), jnp.float32),
            pltpu.SemaphoreType.DMA,
        ],
        compiler_params=params,
    )(band_start, series)
    raw_band = lax.all_to_all(packed_band, AXES, 0, 0, tiled=True).reshape(frames, share_pad)
    packed_own, matrix = pl.pallas_call(
        functools.partial(pack_own_kernel, own),
        out_shape=(
            jax.ShapeDtypeStruct((n_dev, 8, own_pad), jnp.float32),
            jax.ShapeDtypeStruct((kept, frames), jnp.float32),
        ),
        in_specs=[smem, smem, smem, vmem],
        out_specs=(vmem, vmem),
        compiler_params=params,
    )(tap_values, tap_count, kept_frames, series)
    raw_own = lax.all_to_all(packed_own, AXES, 0, 0, tiled=True).reshape(frames, own_pad)
    block = pl.pallas_call(
        scale_band_kernel,
        out_shape=jax.ShapeDtypeStruct((kept, share), jnp.bfloat16),
        in_specs=[vmem, vmem],
        out_specs=vmem,
        compiler_params=params,
    )(matrix, raw_band)

    def swap_row(x, bits):
        return lax.ppermute(x, "row", [(i, i ^ bits) for i in range(n_row)])

    def swap_col(x):
        return lax.ppermute(x, "col", [(0, 1), (1, 0)])

    row, col = lax.axis_index("row"), lax.axis_index("col")
    first = row // 2
    line = jnp.stack([block] + [swap_row(block, 2 * step) for step in range(1, n_quarter)])
    if share % LANES:
        line = jnp.take(line, jnp.arange(n_quarter, dtype=jnp.int32) ^ first, axis=0)
        line = line.transpose(1, 0, 2).reshape(1, kept, n_quarter * share)
        first = jnp.zeros_like(first)
    line_y = swap_row(line, 1)
    line_c = swap_col(line)
    line_yc = swap_col(line_y)

    own_rows = pl.pallas_call(
        scale_own_kernel,
        out_shape=jax.ShapeDtypeStruct((own, kept), jnp.bfloat16),
        in_specs=[vmem, vmem],
        out_specs=vmem,
        compiler_params=params,
    )(matrix, raw_own)
    place = jnp.stack([first, col * 2 + row % 2]).astype(jnp.int32)
    out = fisher_quarter(place, own_rows, line, None, 0)
    out = fisher_quarter(place, own_rows, line_c, out, 2)
    out = fisher_quarter(place, own_rows, line_y, out, 1)
    out = fisher_quarter(place, own_rows, line_yc, out, 3)
    return out.T


def solution(mesh):
    placed = (P(("subj", "row", "col"), None), P(), P(), P("subj"), P("subj"))
    return jax.shard_map(
        body, mesh=mesh, in_specs=placed, out_specs=P("subj", ("row", "col")), check_vma=False
    )
```

```python
import functools

import jax
import jax.numpy as jnp
from jax import lax
from jax.experimental import pallas as pl
from jax.experimental.pallas import tpu as pltpu
from jax.sharding import PartitionSpec as P

B = 4096
LANES = 128
EPSILON = 1e-06
CLIP_LIMIT = 0.999
HALF_LN2 = 0.34657359027997264
N_LOADS = 4
PACK_VMEM = 62 << 20
AXES = ("row", "col")


def round_up(value, unit):
    return (value + unit - 1) // unit * unit


def band_place(device, n_row):
    row, col = device // 2, device % 2
    return (col * 2 + row % 2) * (n_row // 2) + row // 2


def pack_kernel(n_row, own, share, start_ref, series_ref, out_ref, whole_ref, band_ref, sems):
    total = series_ref.shape[1]
    own_pad = round_up(own, LANES)
    tiles = total // LANES
    cuts = [tiles * i // N_LOADS * LANES for i in range(N_LOADS + 1)]
    loads = [
        pltpu.make_async_copy(
            series_ref.at[:, low:high], whole_ref.at[:, low:high], sems.at[i]
        )
        for i, (low, high) in enumerate(zip(cuts, cuts[1:]))
    ]
    for load in loads:
        load.start()
    loaded = 0
    for device in range(2 * n_row):
        while cuts[loaded] < (device + 1) * own:
            loads[loaded].wait()
            loaded += 1
        out_ref[device, :, :own] = whole_ref[:, device * own : (device + 1) * own]
        if own_pad > own:
            out_ref[device, :, own:own_pad] = jnp.zeros((8, own_pad - own), jnp.float32)
    while loaded < N_LOADS:
        loads[loaded].wait()
        loaded += 1

    start = start_ref[0]
    base = pl.multiple_of(jnp.minimum(start // LANES * LANES, total - B - LANES), LANES)
    rest = start - base
    shift = lax.rem(LANES - rest, LANES)
    lane = lax.broadcasted_iota(jnp.int32, (8, LANES), 1)
    here = lane < LANES - rest
    before = pltpu.roll(whole_ref[:, pl.ds(base, LANES)], shift, 1)
    for tile in range(B // LANES):
        after = pltpu.roll(whole_ref[:, pl.ds(base + (tile + 1) * LANES, LANES)], shift, 1)
        band_ref[:, tile * LANES : (tile + 1) * LANES] = jnp.where(here, before, after)
        before = after
    for device in range(2 * n_row):
        place = band_place(device, n_row)
        out_ref[device, :, own_pad : own_pad + share] = band_ref[
            :, place * share : (place + 1) * share
        ]


def filter_matrix(kept, frames, taps_ref, count_ref, kept_ref):
    n_taps = taps_ref.shape[0]
    reach = n_taps // 2
    shape = (kept, LANES)
    place = lax.broadcasted_iota(jnp.int32, shape, 0)

    def skip(block, carry):
        frame, seen = carry
        seen = seen + kept_ref[block]
        return frame + jnp.where(place >= seen, 8 - kept_ref[block], 0), seen

    frame, _ = lax.fori_loop(0, frames // 8, skip, (place, jnp.int32(0)), unroll=frames <= 128)
    reach_used = count_ref[0]
    tap_sum = jnp.float32(0)
    tap_number = jnp.float32(0)
    for tap in range(n_taps):
        used = abs(tap - reach) <= reach_used
        tap_sum = tap_sum + jnp.where(used, taps_ref[tap], 0.0)
        tap_number = tap_number + jnp.where(used, 1.0, 0.0)
    centre = jnp.full(shape, tap_sum, jnp.float32) / jnp.full(shape, tap_number, jnp.float32)
    pieces = []
    for tile in range(frames // LANES):
        offset = lax.broadcasted_iota(jnp.int32, shape, 1) + tile * LANES - frame
        value = jnp.zeros(shape, jnp.float32)
        for tap in range(n_taps):
            value = jnp.where(offset == tap - reach, taps_ref[tap], value)
        pieces.append(jnp.where(jnp.abs(offset) <= reach_used, value - centre, 0.0))
    return pieces[0] if len(pieces) == 1 else jnp.concatenate(pieces, 1)


def matrix_kernel(taps_ref, count_ref, kept_ref, out_ref):
    kept, frames = out_ref.shape
    out_ref[...] = filter_matrix(kept, frames, taps_ref, count_ref, kept_ref)


def scaled_columns(matrix, raw):
    centered = jnp.dot(
        matrix, raw, precision=lax.Precision.HIGHEST, preferred_element_type=jnp.float32
    )
    spread = jnp.sum(centered * centered, axis=0, keepdims=True)
    return centered * lax.rsqrt(spread + EPSILON)


def scale_band_kernel(first, matrix_ref, raw_ref, band_ref):
    scaled = scaled_columns(matrix_ref[...], raw_ref[:, first:])
    band_ref[...] = scaled[:, : band_ref.shape[1]].astype(jnp.bfloat16)


def scale_own_kernel(end, matrix_ref, raw_ref, own_ref):
    scaled = scaled_columns(matrix_ref[...], raw_ref[:, :end])
    own_ref[...] = scaled.T[: own_ref.shape[0]].astype(jnp.bfloat16)


def fisher_kernel(swaps, place_ref, own_ref, *refs):
    lines = refs[: len(swaps)]
    out_ref, made_ref, sems = refs[-3:]
    blocks, _, width = lines[0].shape
    copies = []
    for swap, line_ref in zip(swaps, lines):
        for step in range(blocks):
            spot = len(copies) * width
            correlation = jnp.dot(own_ref[...], line_ref[step], preferred_element_type=jnp.float32)
            c = jnp.clip(correlation, -CLIP_LIMIT, CLIP_LIMIT)
            z_value = HALF_LN2 * (jnp.log2(1.0 + c) - jnp.log2(1.0 - c))
            made_ref[:, spot : spot + width] = z_value.astype(jnp.bfloat16)
            where = ((place_ref[1] ^ swap) * blocks + (place_ref[0] ^ step)) * width
            copy = pltpu.make_async_copy(
                made_ref.at[:, spot : spot + width],
                out_ref.at[:, pl.ds(pl.multiple_of(where, width), width)],
                sems.at[len(copies)],
            )
            copy.start()
            copies.append(copy)
    for copy in copies:
        copy.wait()


def fisher_part(place, own_rows, lines, swaps, out):
    blocks, _, width = lines[0].shape
    own = own_rows.shape[0]
    vmem = pl.BlockSpec(memory_space=pltpu.VMEM)
    specs = [pl.BlockSpec(memory_space=pltpu.SMEM)] + [vmem] * (1 + len(lines))
    args = [place, own_rows, *lines]
    aliases = {}
    if out is not None:
        specs.append(pl.BlockSpec(memory_space=pltpu.HBM))
        aliases = {len(args): 0}
        args.append(out)
    return pl.pallas_call(
        functools.partial(fisher_kernel, swaps),
        out_shape=jax.ShapeDtypeStruct((own, B), jnp.bfloat16),
        in_specs=specs,
        out_specs=pl.BlockSpec(memory_space=pltpu.HBM),
        scratch_shapes=[
            pltpu.VMEM((own, len(lines) * blocks * width), jnp.bfloat16),
            pltpu.SemaphoreType.DMA((len(lines) * blocks,)),
        ],
        input_output_aliases=aliases,
        compiler_params=pltpu.CompilerParams(vmem_limit_bytes=48 << 20),
    )(*args)


def body(series, tap_values, tap_count, kept_frames, band_start):
    n_row = lax.axis_size("row")
    n_dev = n_row * lax.axis_size("col")
    frames = 8 * n_dev
    kept = frames * 3 // 4
    total = series.shape[1]
    own = total // n_dev
    own_pad = round_up(own, LANES)
    share = B // n_dev
    share_pad = round_up(share, LANES)
    n_quarter = n_row // 2
    smem = pl.BlockSpec(memory_space=pltpu.SMEM)
    vmem = pl.BlockSpec(memory_space=pltpu.VMEM)
    params = pltpu.CompilerParams(vmem_limit_bytes=48 << 20)

    packed = pl.pallas_call(
        functools.partial(pack_kernel, n_row, own, share),
        out_shape=jax.ShapeDtypeStruct((n_dev, 8, own_pad + share_pad), jnp.float32),
        in_specs=[smem, pl.BlockSpec(memory_space=pltpu.HBM)],
        out_specs=vmem,
        scratch_shapes=[
            pltpu.VMEM((8, total), jnp.float32),
            pltpu.VMEM((8, B), jnp.float32),
            pltpu.SemaphoreType.DMA((N_LOADS,)),
        ],
        compiler_params=pltpu.CompilerParams(vmem_limit_bytes=PACK_VMEM),
    )(band_start, series)
    raw = lax.all_to_all(packed, AXES, 0, 0, tiled=True).reshape(frames, own_pad + share_pad)
    matrix = pl.pallas_call(
        matrix_kernel,
        out_shape=jax.ShapeDtypeStruct((kept, frames), jnp.float32),
        in_specs=[smem, smem, smem],
        out_specs=vmem,
        compiler_params=params,
    )(tap_values, tap_count, kept_frames)
    block = pl.pallas_call(
        functools.partial(scale_band_kernel, own_pad),
        out_shape=jax.ShapeDtypeStruct((kept, share), jnp.bfloat16),
        in_specs=[vmem, vmem],
        out_specs=vmem,
        compiler_params=params,
    )(matrix, raw)

    def swap_row(x, bits):
        return lax.ppermute(x, "row", [(i, i ^ bits) for i in range(n_row)])

    def swap_col(x):
        return lax.ppermute(x, "col", [(0, 1), (1, 0)])

    row, col = lax.axis_index("row"), lax.axis_index("col")
    first = row // 2
    own_rows = pl.pallas_call(
        functools.partial(scale_own_kernel, own_pad),
        out_shape=jax.ShapeDtypeStruct((own, kept), jnp.bfloat16),
        in_specs=[vmem, vmem],
        out_specs=vmem,
        compiler_params=params,
    )(matrix, raw)
    parts = [block] + [swap_row(block, 2 * step) for step in range(1, n_quarter)]
    own_rows, *parts = lax.optimization_barrier((own_rows, *parts))
    line = jnp.stack(parts)
    if share % LANES:
        line = jnp.take(line, jnp.arange(n_quarter, dtype=jnp.int32) ^ first, axis=0)
        line = line.transpose(1, 0, 2).reshape(1, kept, n_quarter * share)
        first = jnp.zeros_like(first)
    place = jnp.stack([first, col * 2 + row % 2]).astype(jnp.int32)
    line_y = swap_row(line, 1)
    line_c = swap_col(line)
    out = fisher_part(place, own_rows, [line, line_c], (0, 2), None)
    line_y, out = lax.optimization_barrier((line_y, out))
    line_yc = swap_col(line_y)
    out = fisher_part(place, own_rows, [line_y, line_yc], (1, 3), out)
    return out.T


def solution(mesh):
    placed = (P(("subj", "row", "col"), None), P(), P(), P("subj"), P("subj"))
    return jax.shard_map(
        body, mesh=mesh, in_specs=placed, out_specs=P("subj", ("row", "col")), check_vma=False
    )
```

```python
import functools

import jax
import jax.numpy as jnp
from jax import lax
from jax.experimental import pallas as pl
from jax.experimental.pallas import tpu as pltpu
from jax.sharding import PartitionSpec as P

B = 4096
LANES = 128
EPSILON = 1e-06
CLIP_LIMIT = 0.999
HALF_LN2 = 0.34657359027997264
N_LOADS = 4
PACK_VMEM = 62 << 20
AXES = ("row", "col")


def round_up(value, unit):
    return (value + unit - 1) // unit * unit


def band_place(device, n_row):
    row, col = device // 2, device % 2
    return (col * 2 + row % 2) * (n_row // 2) + row // 2


def pack_kernel(
    n_row, own, share, start_ref, series_ref, out_ref, whole_ref, own_ref, band_ref, shares_ref, load_sems, sems
):
    total = series_ref.shape[1]
    n_dev = 2 * n_row
    own_pad = own_ref.shape[2]
    tiles = total // LANES
    cuts = [tiles * i // N_LOADS * LANES for i in range(N_LOADS + 1)]
    loads = [
        pltpu.make_async_copy(
            series_ref.at[:, low:high], whole_ref.at[:, low:high], load_sems.at[i]
        )
        for i, (low, high) in enumerate(zip(cuts, cuts[1:]))
    ]
    for load in loads:
        load.start()
    loaded = 0
    stores = []
    for device in range(n_dev):
        while cuts[loaded] < (device + 1) * own:
            loads[loaded].wait()
            loaded += 1
        own_ref[device, :, :own] = whole_ref[:, device * own : (device + 1) * own]
        if own_pad > own:
            own_ref[device, :, own:] = jnp.zeros((8, own_pad - own), jnp.float32)
        store = pltpu.make_async_copy(
            own_ref.at[device], out_ref.at[device, :, :own_pad], sems.at[device]
        )
        store.start()
        stores.append(store)
    while loaded < N_LOADS:
        loads[loaded].wait()
        loaded += 1

    start = start_ref[0]
    base = pl.multiple_of(jnp.minimum(start // LANES * LANES, total - B - LANES), LANES)
    rest = start - base
    shift = lax.rem(LANES - rest, LANES)
    lane = lax.broadcasted_iota(jnp.int32, (8, LANES), 1)
    here = lane < LANES - rest
    before = pltpu.roll(whole_ref[:, pl.ds(base, LANES)], shift, 1)
    for tile in range(B // LANES):
        after = pltpu.roll(whole_ref[:, pl.ds(base + (tile + 1) * LANES, LANES)], shift, 1)
        band_ref[:, tile * LANES : (tile + 1) * LANES] = jnp.where(here, before, after)
        before = after
    for device in range(n_dev):
        place = band_place(device, n_row)
        shares_ref[device, :, :share] = band_ref[:, place * share : (place + 1) * share]
    store = pltpu.make_async_copy(shares_ref, out_ref.at[:, :, own_pad:], sems.at[n_dev])
    store.start()
    stores.append(store)
    for store in stores:
        store.wait()


def filter_matrix(kept, frames, taps_ref, count_ref, kept_ref):
    n_taps = taps_ref.shape[0]
    reach = n_taps // 2
    shape = (kept, LANES)
    place = lax.broadcasted_iota(jnp.int32, shape, 0)

    def skip(block, carry):
        frame, seen = carry
        seen = seen + kept_ref[block]
        return frame + jnp.where(place >= seen, 8 - kept_ref[block], 0), seen

    frame, _ = lax.fori_loop(0, frames // 8, skip, (place, jnp.int32(0)), unroll=frames <= 128)
    reach_used = count_ref[0]
    tap_sum = jnp.float32(0)
    tap_number = jnp.float32(0)
    for tap in range(n_taps):
        used = abs(tap - reach) <= reach_used
        tap_sum = tap_sum + jnp.where(used, taps_ref[tap], 0.0)
        tap_number = tap_number + jnp.where(used, 1.0, 0.0)
    centre = jnp.full(shape, tap_sum, jnp.float32) / jnp.full(shape, tap_number, jnp.float32)
    pieces = []
    for tile in range(frames // LANES):
        offset = lax.broadcasted_iota(jnp.int32, shape, 1) + tile * LANES - frame
        value = jnp.zeros(shape, jnp.float32)
        for tap in range(n_taps):
            value = jnp.where(offset == tap - reach, taps_ref[tap], value)
        pieces.append(jnp.where(jnp.abs(offset) <= reach_used, value - centre, 0.0))
    return pieces[0] if len(pieces) == 1 else jnp.concatenate(pieces, 1)


def matrix_kernel(taps_ref, count_ref, kept_ref, out_ref):
    kept, frames = out_ref.shape
    out_ref[...] = filter_matrix(kept, frames, taps_ref, count_ref, kept_ref)


def scaled_columns(matrix, raw):
    centered = jnp.dot(
        matrix, raw, precision=lax.Precision.HIGHEST, preferred_element_type=jnp.float32
    )
    spread = jnp.sum(centered * centered, axis=0, keepdims=True)
    return centered * lax.rsqrt(spread + EPSILON)


def scale_band_kernel(first, matrix_ref, raw_ref, band_ref):
    scaled = scaled_columns(matrix_ref[...], raw_ref[:, first:])
    band_ref[...] = scaled[:, : band_ref.shape[1]].astype(jnp.bfloat16)


def scale_own_kernel(end, matrix_ref, raw_ref, own_ref):
    scaled = scaled_columns(matrix_ref[...], raw_ref[:, :end])
    own_ref[...] = scaled.T[: own_ref.shape[0]].astype(jnp.bfloat16)


def fisher_kernel(spots, n_blocks, place_ref, own_ref, *refs):
    pieces = refs[: len(spots)]
    out_ref, made_ref, sems = refs[-3:]
    width = pieces[0].shape[2]
    copies = []
    for (swap, steps), piece_ref in zip(spots, pieces):
        for at, step in enumerate(steps):
            spot = len(copies) * width
            correlation = jnp.dot(own_ref[...], piece_ref[at], preferred_element_type=jnp.float32)
            c = jnp.clip(correlation, -CLIP_LIMIT, CLIP_LIMIT)
            z_value = HALF_LN2 * (jnp.log2(1.0 + c) - jnp.log2(1.0 - c))
            made_ref[:, spot : spot + width] = z_value.astype(jnp.bfloat16)
            where = ((place_ref[1] ^ swap) * n_blocks + (place_ref[0] ^ step)) * width
            copy = pltpu.make_async_copy(
                made_ref.at[:, spot : spot + width],
                out_ref.at[:, pl.ds(pl.multiple_of(where, width), width)],
                sems.at[len(copies)],
            )
            copy.start()
            copies.append(copy)
    for copy in copies:
        copy.wait()


def fisher_part(n_blocks, place, own_rows, pieces, out):
    spots = [(swap, steps) for swap, steps, _ in pieces]
    arrays = [array for _, _, array in pieces]
    count, width = sum(len(steps) for _, steps in spots), arrays[0].shape[2]
    own = own_rows.shape[0]
    vmem = pl.BlockSpec(memory_space=pltpu.VMEM)
    specs = [pl.BlockSpec(memory_space=pltpu.SMEM)] + [vmem] * (1 + len(arrays))
    args = [place, own_rows, *arrays]
    aliases = {}
    if out is not None:
        specs.append(pl.BlockSpec(memory_space=pltpu.HBM))
        aliases = {len(args): 0}
        args.append(out)
    return pl.pallas_call(
        functools.partial(fisher_kernel, spots, n_blocks),
        out_shape=jax.ShapeDtypeStruct((own, B), jnp.bfloat16),
        in_specs=specs,
        out_specs=pl.BlockSpec(memory_space=pltpu.HBM),
        scratch_shapes=[
            pltpu.VMEM((own, count * width), jnp.bfloat16),
            pltpu.SemaphoreType.DMA((count,)),
        ],
        input_output_aliases=aliases,
        compiler_params=pltpu.CompilerParams(vmem_limit_bytes=48 << 20),
    )(*args)


def body(series, tap_values, tap_count, kept_frames, band_start):
    n_row = lax.axis_size("row")
    n_dev = n_row * lax.axis_size("col")
    frames = 8 * n_dev
    kept = frames * 3 // 4
    total = series.shape[1]
    own = total // n_dev
    own_pad = round_up(own, LANES)
    share = B // n_dev
    share_pad = round_up(share, LANES)
    n_quarter = n_row // 2
    smem = pl.BlockSpec(memory_space=pltpu.SMEM)
    vmem = pl.BlockSpec(memory_space=pltpu.VMEM)
    params = pltpu.CompilerParams(vmem_limit_bytes=48 << 20)

    hbm = pl.BlockSpec(memory_space=pltpu.HBM)
    packed = pl.pallas_call(
        functools.partial(pack_kernel, n_row, own, share),
        out_shape=jax.ShapeDtypeStruct((n_dev, 8, own_pad + share_pad), jnp.float32),
        in_specs=[smem, hbm],
        out_specs=hbm,
        scratch_shapes=[
            pltpu.VMEM((8, total), jnp.float32),
            pltpu.VMEM((n_dev, 8, own_pad), jnp.float32),
            pltpu.VMEM((8, B), jnp.float32),
            pltpu.VMEM((n_dev, 8, share_pad), jnp.float32),
            pltpu.SemaphoreType.DMA((N_LOADS,)),
            pltpu.SemaphoreType.DMA((n_dev + 1,)),
        ],
        compiler_params=pltpu.CompilerParams(vmem_limit_bytes=PACK_VMEM),
    )(band_start, series)
    raw = lax.all_to_all(packed, AXES, 0, 0, tiled=True).reshape(frames, own_pad + share_pad)
    matrix = pl.pallas_call(
        matrix_kernel,
        out_shape=jax.ShapeDtypeStruct((kept, frames), jnp.float32),
        in_specs=[smem, smem, smem],
        out_specs=vmem,
        compiler_params=params,
    )(tap_values, tap_count, kept_frames)
    block = pl.pallas_call(
        functools.partial(scale_band_kernel, own_pad),
        out_shape=jax.ShapeDtypeStruct((kept, share), jnp.bfloat16),
        in_specs=[vmem, vmem],
        out_specs=vmem,
        compiler_params=params,
    )(matrix, raw)

    def swap_row(x, bits):
        return lax.ppermute(x, "row", [(i, i ^ bits) for i in range(n_row)])

    def swap_col(x):
        return lax.ppermute(x, "col", [(0, 1), (1, 0)])

    row, col = lax.axis_index("row"), lax.axis_index("col")
    first = row // 2
    own_rows = pl.pallas_call(
        functools.partial(scale_own_kernel, own_pad),
        out_shape=jax.ShapeDtypeStruct((own, kept), jnp.bfloat16),
        in_specs=[vmem, vmem],
        out_specs=vmem,
        compiler_params=params,
    )(matrix, raw)
    arrived = {step: swap_row(block, 2 * step) for step in reversed(range(1, n_quarter))}
    arrived[0] = block
    if share % LANES:
        line = jnp.stack([arrived[step] for step in range(n_quarter)])
        line = jnp.take(line, jnp.arange(n_quarter, dtype=jnp.int32) ^ first, axis=0)
        near = line.transpose(1, 0, 2).reshape(1, kept, n_quarter * share)
        first = jnp.zeros_like(first)
        pieces = [((0,), near)]
        n_blocks = 1
    else:
        half = n_quarter // 2
        pieces = [
            (steps, jnp.stack([arrived[step] for step in steps]))
            for steps in (tuple(range(half)), tuple(range(half, n_quarter)))
        ]
        n_blocks = n_quarter
    place = jnp.stack([first, col * 2 + row % 2]).astype(jnp.int32)
    near_steps, near = pieces[0]
    near_y = swap_row(near, 1)
    fars = [(steps, far, swap_row(far, 1)) for steps, far in pieces[1:]]
    late = [(2, near_steps, swap_col(near)), (3, near_steps, swap_col(near_y))]
    late += [(2, steps, swap_col(far)) for steps, far, _ in fars]
    early = [(0, near_steps, near), (1, near_steps, near_y)]
    early += [(0, steps, far) for steps, far, _ in fars]
    out = fisher_part(n_blocks, place, own_rows, early, None)
    for steps, _, far_y in fars:
        far_y, out = lax.optimization_barrier((far_y, out))
        late += [(1, steps, far_y), (3, steps, swap_col(far_y))]
    out = fisher_part(n_blocks, place, own_rows, late, out)
    return out.T


def solution(mesh):
    placed = (P(("subj", "row", "col"), None), P(), P(), P("subj"), P("subj"))
    return jax.shard_map(
        body, mesh=mesh, in_specs=placed, out_specs=P("subj", ("row", "col")), check_vma=False
    )
```

```python
import functools

import jax
import jax.numpy as jnp
from jax import lax
from jax.experimental import pallas as pl
from jax.experimental.pallas import tpu as pltpu
from jax.sharding import PartitionSpec as P

B = 4096
LANES = 128
EPSILON = 1e-06
CLIP_LIMIT = 0.999
HALF_LN2 = 0.34657359027997264
N_LOADS = 4
GROUP = 8
PACK_VMEM = 62 << 20
AXES = ("row", "col")


def round_up(value, unit):
    return (value + unit - 1) // unit * unit


def band_place(device):
    row, col = device // 2, device % 2
    return col * 4 + row % 4


def pack_kernel(
    own, start_ref, series_ref, out_ref, whole_ref, own_ref, band_ref, load_sems, own_sems, band_sems
):
    total = series_ref.shape[1]
    n_dev, _, own_pad = own_ref.shape
    share = B // GROUP
    tiles = total // LANES
    cuts = [tiles * i // N_LOADS * LANES for i in range(N_LOADS + 1)]
    loads = [
        pltpu.make_async_copy(
            series_ref.at[:, low:high], whole_ref.at[:, low:high], load_sems.at[i]
        )
        for i, (low, high) in enumerate(zip(cuts, cuts[1:]))
    ]
    for load in loads:
        load.start()
    loaded = 0
    stores = []
    for device in range(n_dev):
        while cuts[loaded] < (device + 1) * own:
            loads[loaded].wait()
            loaded += 1
        own_ref[device, :, :own] = whole_ref[:, device * own : (device + 1) * own]
        if own_pad > own:
            own_ref[device, :, own:] = jnp.zeros((8, own_pad - own), jnp.float32)
        store = pltpu.make_async_copy(
            own_ref.at[device], out_ref.at[device, :, :own_pad], own_sems.at[device]
        )
        store.start()
        stores.append(store)
    while loaded < N_LOADS:
        loads[loaded].wait()
        loaded += 1

    start = start_ref[0]
    base = pl.multiple_of(jnp.minimum(start // LANES * LANES, total - B - LANES), LANES)
    rest = start - base
    shift = lax.rem(LANES - rest, LANES)
    lane = lax.broadcasted_iota(jnp.int32, (8, LANES), 1)
    here = lane < LANES - rest
    before = pltpu.roll(whole_ref[:, pl.ds(base, LANES)], shift, 1)
    for tile in range(B // LANES):
        after = pltpu.roll(whole_ref[:, pl.ds(base + (tile + 1) * LANES, LANES)], shift, 1)
        band_ref[:, tile * LANES : (tile + 1) * LANES] = jnp.where(here, before, after)
        before = after
    for device in range(n_dev):
        place = band_place(device)
        store = pltpu.make_async_copy(
            band_ref.at[:, place * share : (place + 1) * share],
            out_ref.at[device, :, own_pad:],
            band_sems.at[device],
        )
        store.start()
        stores.append(store)
    for store in stores:
        store.wait()


def filter_matrix(kept, frames, taps_ref, count_ref, kept_ref):
    n_taps = taps_ref.shape[0]
    reach = n_taps // 2
    shape = (kept, LANES)
    place = lax.broadcasted_iota(jnp.int32, shape, 0)

    def skip(block, carry):
        frame, seen = carry
        seen = seen + kept_ref[block]
        return frame + jnp.where(place >= seen, 8 - kept_ref[block], 0), seen

    frame, _ = lax.fori_loop(0, frames // 8, skip, (place, jnp.int32(0)), unroll=frames <= 128)
    reach_used = count_ref[0]
    tap_sum = jnp.float32(0)
    tap_number = jnp.float32(0)
    for tap in range(n_taps):
        used = abs(tap - reach) <= reach_used
        tap_sum = tap_sum + jnp.where(used, taps_ref[tap], 0.0)
        tap_number = tap_number + jnp.where(used, 1.0, 0.0)
    centre = jnp.full(shape, tap_sum, jnp.float32) / jnp.full(shape, tap_number, jnp.float32)
    pieces = []
    for tile in range(frames // LANES):
        offset = lax.broadcasted_iota(jnp.int32, shape, 1) + tile * LANES - frame
        value = jnp.zeros(shape, jnp.float32)
        for tap in range(n_taps):
            value = jnp.where(offset == tap - reach, taps_ref[tap], value)
        pieces.append(jnp.where(jnp.abs(offset) <= reach_used, value - centre, 0.0))
    return pieces[0] if len(pieces) == 1 else jnp.concatenate(pieces, 1)


def matrix_kernel(taps_ref, count_ref, kept_ref, out_ref):
    kept, frames = out_ref.shape
    out_ref[...] = filter_matrix(kept, frames, taps_ref, count_ref, kept_ref)


def scaled_columns(matrix, raw):
    centered = jnp.dot(
        matrix, raw, precision=lax.Precision.HIGHEST, preferred_element_type=jnp.float32
    )
    spread = jnp.sum(centered * centered, axis=0, keepdims=True)
    return centered * lax.rsqrt(spread + EPSILON)


def scale_band_kernel(first, matrix_ref, raw_ref, band_ref):
    scaled = scaled_columns(matrix_ref[...], raw_ref[:, first:])
    band_ref[...] = scaled[:, : band_ref.shape[1]].astype(jnp.bfloat16)


def scale_own_kernel(end, matrix_ref, raw_ref, own_ref):
    scaled = scaled_columns(matrix_ref[...], raw_ref[:, :end])
    own_ref[...] = scaled.T[: own_ref.shape[0]].astype(jnp.bfloat16)


def fisher_kernel(flips, place_ref, own_ref, *refs):
    pieces = refs[: len(flips)]
    out_ref, made_ref, sems = refs[-3:]
    share = pieces[0].shape[1]
    half = share // 2
    copies = []
    for at, (flip, piece_ref) in enumerate(zip(flips, pieces)):
        for low in (0, half):
            correlation = jnp.dot(
                own_ref[...], piece_ref[:, low : low + half], preferred_element_type=jnp.float32
            )
            c = jnp.clip(correlation, -CLIP_LIMIT, CLIP_LIMIT)
            z_value = HALF_LN2 * (jnp.log2(1.0 + c) - jnp.log2(1.0 - c))
            made_ref[:, at * share + low : at * share + low + half] = z_value.astype(jnp.bfloat16)
        where = pl.multiple_of((place_ref[0] ^ flip) * share, share)
        copy = pltpu.make_async_copy(
            made_ref.at[:, at * share : (at + 1) * share],
            out_ref.at[:, pl.ds(where, share)],
            sems.at[at],
        )
        copy.start()
        copies.append(copy)
    for copy in copies:
        copy.wait()


def fisher_part(place, own_rows, pieces, out):
    flips = [flip for flip, _ in pieces]
    arrays = [array for _, array in pieces]
    own = own_rows.shape[0]
    vmem = pl.BlockSpec(memory_space=pltpu.VMEM)
    specs = [pl.BlockSpec(memory_space=pltpu.SMEM)] + [vmem] * (1 + len(arrays))
    args = [place, own_rows, *arrays]
    aliases = {}
    if out is not None:
        specs.append(pl.BlockSpec(memory_space=pltpu.HBM))
        aliases = {len(args): 0}
        args.append(out)
    return pl.pallas_call(
        functools.partial(fisher_kernel, flips),
        out_shape=jax.ShapeDtypeStruct((own, B), jnp.bfloat16),
        in_specs=specs,
        out_specs=pl.BlockSpec(memory_space=pltpu.HBM),
        scratch_shapes=[
            pltpu.VMEM((own, len(arrays) * arrays[0].shape[1]), jnp.bfloat16),
            pltpu.SemaphoreType.DMA((len(arrays),)),
        ],
        input_output_aliases=aliases,
        compiler_params=pltpu.CompilerParams(vmem_limit_bytes=48 << 20),
    )(*args)


def body(series, tap_values, tap_count, kept_frames, band_start):
    n_row = lax.axis_size("row")
    n_dev = n_row * lax.axis_size("col")
    frames = 8 * n_dev
    kept = frames * 3 // 4
    total = series.shape[1]
    own = total // n_dev
    own_pad = round_up(own, LANES)
    share = B // GROUP
    smem = pl.BlockSpec(memory_space=pltpu.SMEM)
    vmem = pl.BlockSpec(memory_space=pltpu.VMEM)
    hbm = pl.BlockSpec(memory_space=pltpu.HBM)
    params = pltpu.CompilerParams(vmem_limit_bytes=48 << 20)

    packed = pl.pallas_call(
        functools.partial(pack_kernel, own),
        out_shape=jax.ShapeDtypeStruct((n_dev, 8, own_pad + share), jnp.float32),
        in_specs=[smem, hbm],
        out_specs=hbm,
        scratch_shapes=[
            pltpu.VMEM((8, total), jnp.float32),
            pltpu.VMEM((n_dev, 8, own_pad), jnp.float32),
            pltpu.VMEM((8, B), jnp.float32),
            pltpu.SemaphoreType.DMA((N_LOADS,)),
            pltpu.SemaphoreType.DMA((n_dev,)),
            pltpu.SemaphoreType.DMA((n_dev,)),
        ],
        compiler_params=pltpu.CompilerParams(vmem_limit_bytes=PACK_VMEM),
    )(band_start, series)
    raw = lax.all_to_all(packed, AXES, 0, 0, tiled=True).reshape(frames, own_pad + share)
    matrix = pl.pallas_call(
        matrix_kernel,
        out_shape=jax.ShapeDtypeStruct((kept, frames), jnp.float32),
        in_specs=[smem, smem, smem],
        out_specs=vmem,
        compiler_params=params,
    )(tap_values, tap_count, kept_frames)
    block = pl.pallas_call(
        functools.partial(scale_band_kernel, own_pad),
        out_shape=jax.ShapeDtypeStruct((kept, share), jnp.bfloat16),
        in_specs=[vmem, vmem],
        out_specs=vmem,
        compiler_params=params,
    )(matrix, raw)
    own_rows = pl.pallas_call(
        functools.partial(scale_own_kernel, own_pad),
        out_shape=jax.ShapeDtypeStruct((own, kept), jnp.bfloat16),
        in_specs=[vmem, vmem],
        out_specs=vmem,
        compiler_params=params,
    )(matrix, raw)

    def swap_row(x, bits):
        return lax.ppermute(x, "row", [(i, i ^ bits) for i in range(n_row)])

    def swap_col(x):
        return lax.ppermute(x, "col", [(0, 1), (1, 0)])

    place = (lax.axis_index("col") * 4 + lax.axis_index("row") % 4).astype(jnp.int32).reshape(1)
    near = swap_row(block, 2)
    side = swap_row(block, 1)
    across = swap_row(block, 3)
    early = [(0, block), (4, swap_col(block)), (2, near)]
    out = fisher_part(place, own_rows, early, None)
    side, across, out = lax.optimization_barrier((side, across, out))
    late = [(6, swap_col(near)), (1, side), (3, across), (5, swap_col(side)), (7, swap_col(across))]
    out = fisher_part(place, own_rows, late, out)
    return out.T


def solution(mesh):
    placed = (P(("subj", "row", "col"), None), P(), P(), P("subj"), P("subj"))
    return jax.shard_map(
        body, mesh=mesh, in_specs=placed, out_specs=P("subj", ("row", "col")), check_vma=False
    )
```

```python
import functools

import jax
import jax.numpy as jnp
import numpy as np
from jax import lax
from jax.experimental import pallas as pl
from jax.experimental.pallas import tpu as pltpu
from jax.sharding import PartitionSpec as P

B = 4096
LANES = 128
EPSILON = 1e-06
CLIP_LIMIT = 0.999
HALF_LN2 = 0.34657359027997264
GROUP = 8
AXES = ("row", "col")


def round_up(value, unit):
    return (value + unit - 1) // unit * unit


def band_place(device):
    row, col = device // 2, device % 2
    return col * 4 + row % 4


def shift_band(start_ref, series_ref, band_ref):
    total = series_ref.shape[1]
    start = start_ref[0]
    base = pl.multiple_of(jnp.minimum(start // LANES * LANES, total - B - LANES), LANES)
    rest = start - base
    shift = lax.rem(LANES - rest, LANES)
    lane = lax.broadcasted_iota(jnp.int32, (8, LANES), 1)
    here = lane < LANES - rest
    before = pltpu.roll(series_ref[:, pl.ds(base, LANES)], shift, 1)
    for tile in range(B // LANES):
        after = pltpu.roll(series_ref[:, pl.ds(base + (tile + 1) * LANES, LANES)], shift, 1)
        band_ref[:, tile * LANES : (tile + 1) * LANES] = jnp.where(here, before, after)
        before = after


def own_columns(device, own, own_pad, series_ref):
    columns = series_ref[:, device * own : (device + 1) * own]
    if own_pad > own:
        columns = jnp.concatenate([columns, jnp.zeros((8, own_pad - own), jnp.float32)], 1)
    return columns


def pack_all_kernel(own, start_ref, series_ref, out_ref, band_ref):
    share = B // GROUP
    own_pad = out_ref.shape[2] - share
    shift_band(start_ref, series_ref, band_ref)
    for device in range(out_ref.shape[0]):
        out_ref[device, :, :own_pad] = own_columns(device, own, own_pad, series_ref)
        place = band_place(device)
        out_ref[device, :, own_pad:] = band_ref[:, place * share : (place + 1) * share]


def pack_kernel(own, start_ref, series_ref, straight_ref, cross_ref, band_ref):
    share = B // GROUP
    own_pad = straight_ref.shape[2] - share
    first_core = lax.axis_index("col") == 0
    shift_band(start_ref, series_ref, band_ref)
    for row in range(straight_ref.shape[0]):
        slabs = []
        for device in (2 * row, 2 * row + 1):
            place = band_place(device)
            slabs.append(
                (
                    own_columns(device, own, own_pad, series_ref),
                    band_ref[:, place * share : (place + 1) * share],
                )
            )
        for (low, high), zero, one in zip(((0, own_pad), (own_pad, own_pad + share)), *slabs):
            straight_ref[row, :, low:high] = jnp.where(first_core, zero, one)
            cross_ref[row, :, low:high] = jnp.where(first_core, one, zero)


def merge_kernel(straight_ref, crossed_ref, *out_refs):
    row = lax.axis_index("row")
    for mask, out_ref in enumerate(out_refs):
        out_ref[:8] = straight_ref[row ^ mask]
        out_ref[8:] = crossed_ref[row ^ mask]


def filter_matrix(kept, frames, turn, taps_ref, count_ref, kept_ref):
    n_taps = taps_ref.shape[0]
    reach = n_taps // 2
    shape = (kept, LANES)
    place = lax.broadcasted_iota(jnp.int32, shape, 0)

    def skip(block, carry):
        frame, seen = carry
        seen = seen + kept_ref[block]
        return frame + jnp.where(place >= seen, 8 - kept_ref[block], 0), seen

    frame, _ = lax.fori_loop(0, frames // 8, skip, (place, jnp.int32(0)), unroll=frames <= 128)
    reach_used = count_ref[0]
    tap_sum = jnp.float32(0)
    tap_number = jnp.float32(0)
    for tap in range(n_taps):
        used = abs(tap - reach) <= reach_used
        tap_sum = tap_sum + jnp.where(used, taps_ref[tap], 0.0)
        tap_number = tap_number + jnp.where(used, 1.0, 0.0)
    centre = jnp.full(shape, tap_sum, jnp.float32) / jnp.full(shape, tap_number, jnp.float32)
    pieces = []
    for tile in range(frames // LANES):
        offset = ((lax.broadcasted_iota(jnp.int32, shape, 1) + tile * LANES) ^ turn) - frame
        value = jnp.zeros(shape, jnp.float32)
        for tap in range(n_taps):
            value = jnp.where(offset == tap - reach, taps_ref[tap], value)
        pieces.append(jnp.where(jnp.abs(offset) <= reach_used, value - centre, 0.0))
    return pieces[0] if len(pieces) == 1 else jnp.concatenate(pieces, 1)


def matrix_kernel(relative, taps_ref, count_ref, kept_ref, out_ref):
    kept, frames = out_ref.shape
    turn = 8 * (2 * lax.axis_index("row") + lax.axis_index("col")) if relative else 0
    out_ref[...] = filter_matrix(kept, frames, turn, taps_ref, count_ref, kept_ref)


def scaled_columns(matrix, raw):
    centered = jnp.dot(
        matrix, raw, precision=lax.Precision.HIGHEST, preferred_element_type=jnp.float32
    )
    spread = jnp.sum(centered * centered, axis=0, keepdims=True)
    return centered * lax.rsqrt(spread + EPSILON)


def scale_band_kernel(masks, first, matrix_ref, *refs):
    *raw_refs, band_ref = refs
    raw = jnp.concatenate([raw_refs[i][:, first:] for i in np.argsort(masks)], 0)
    band_ref[...] = scaled_columns(matrix_ref[...], raw).astype(jnp.bfloat16)


def scale_own_kernel(masks, end, matrix_ref, *refs):
    *raw_refs, own_ref = refs
    raw = jnp.concatenate([raw_refs[i][:, :end] for i in np.argsort(masks)], 0)
    scaled = scaled_columns(matrix_ref[...], raw)
    own_ref[...] = scaled.T[: own_ref.shape[0]].astype(jnp.bfloat16)


def fisher_kernel(flips, own_ref, *refs):
    pieces = refs[: len(flips)]
    out_ref, made_ref, sems = refs[-3:]
    share = pieces[0].shape[1]
    half = share // 2
    place = lax.axis_index("col") * 4 + lax.axis_index("row") % 4
    copies = []
    for at, (flip, piece_ref) in enumerate(zip(flips, pieces)):
        for low in (0, half):
            correlation = jnp.dot(
                own_ref[...], piece_ref[:, low : low + half], preferred_element_type=jnp.float32
            )
            c = jnp.clip(correlation, -CLIP_LIMIT, CLIP_LIMIT)
            z_value = HALF_LN2 * (jnp.log2(1.0 + c) - jnp.log2(1.0 - c))
            made_ref[:, at * share + low : at * share + low + half] = z_value.astype(jnp.bfloat16)
        where = pl.multiple_of((place ^ flip) * share, share)
        copy = pltpu.make_async_copy(
            made_ref.at[:, at * share : (at + 1) * share],
            out_ref.at[:, pl.ds(where, share)],
            sems.at[at],
        )
        copy.start()
        copies.append(copy)
    for copy in copies:
        copy.wait()


def fisher_part(own_rows, pieces, out):
    flips = [flip for flip, _ in pieces]
    arrays = [array for _, array in pieces]
    own = own_rows.shape[0]
    vmem = pl.BlockSpec(memory_space=pltpu.VMEM)
    specs = [vmem] * (1 + len(arrays))
    args = [own_rows, *arrays]
    aliases = {}
    if out is not None:
        specs.append(pl.BlockSpec(memory_space=pltpu.HBM))
        aliases = {len(args): 0}
        args.append(out)
    return pl.pallas_call(
        functools.partial(fisher_kernel, flips),
        out_shape=jax.ShapeDtypeStruct((own, B), jnp.bfloat16),
        in_specs=specs,
        out_specs=pl.BlockSpec(memory_space=pltpu.HBM),
        scratch_shapes=[
            pltpu.VMEM((own, len(arrays) * arrays[0].shape[1]), jnp.bfloat16),
            pltpu.SemaphoreType.DMA((len(arrays),)),
        ],
        input_output_aliases=aliases,
        compiler_params=pltpu.CompilerParams(vmem_limit_bytes=48 << 20),
    )(*args)


def body(series, tap_values, tap_count, kept_frames, band_start):
    n_row = lax.axis_size("row")
    n_dev = n_row * lax.axis_size("col")
    frames = 8 * n_dev
    kept = frames * 3 // 4
    total = series.shape[1]
    own = total // n_dev
    own_pad = round_up(own, LANES)
    share = B // GROUP
    smem = pl.BlockSpec(memory_space=pltpu.SMEM)
    vmem = pl.BlockSpec(memory_space=pltpu.VMEM)
    params = pltpu.CompilerParams(vmem_limit_bytes=24 << 20)
    width = own_pad + share

    def swap_row(x, bits):
        return lax.ppermute(x, "row", [(i, i ^ bits) for i in range(n_row)])

    def swap_col(x):
        return lax.ppermute(x, "col", [(0, 1), (1, 0)])

    relative = n_row <= 8
    matrix = pl.pallas_call(
        functools.partial(matrix_kernel, relative),
        out_shape=jax.ShapeDtypeStruct((kept, frames), jnp.float32),
        in_specs=[smem, smem, smem],
        out_specs=vmem,
        compiler_params=params,
    )(tap_values, tap_count, kept_frames)
    if relative:
        slabs = jax.ShapeDtypeStruct((n_row, 8, width), jnp.float32)
        straight, cross = pl.pallas_call(
            functools.partial(pack_kernel, own),
            out_shape=(slabs, slabs),
            in_specs=[smem, vmem],
            out_specs=(vmem, vmem),
            scratch_shapes=[pltpu.VMEM((8, B), jnp.float32)],
            compiler_params=params,
        )(band_start, series)
        raws = list(pl.pallas_call(
            merge_kernel,
            out_shape=[jax.ShapeDtypeStruct((16, width), jnp.float32)] * n_row,
            in_specs=[vmem, vmem],
            out_specs=[vmem] * n_row,
            compiler_params=params,
        )(straight, swap_col(cross)))
        masks = [*range(n_row // 2, n_row), *range(n_row // 2)]
        raws = [swap_row(raws[mask], mask) if mask else raws[0] for mask in masks]
    else:
        packed = pl.pallas_call(
            functools.partial(pack_all_kernel, own),
            out_shape=jax.ShapeDtypeStruct((n_dev, 8, width), jnp.float32),
            in_specs=[smem, vmem],
            out_specs=vmem,
            scratch_shapes=[pltpu.VMEM((8, B), jnp.float32)],
            compiler_params=params,
        )(band_start, series)
        masks = [0]
        raws = [lax.all_to_all(packed, AXES, 0, 0, tiled=True).reshape(frames, width)]
    block = pl.pallas_call(
        functools.partial(scale_band_kernel, masks, own_pad),
        out_shape=jax.ShapeDtypeStruct((kept, share), jnp.bfloat16),
        in_specs=[vmem] * (1 + len(raws)),
        out_specs=vmem,
        compiler_params=params,
    )(matrix, *raws)
    own_rows = pl.pallas_call(
        functools.partial(scale_own_kernel, masks, own_pad),
        out_shape=jax.ShapeDtypeStruct((own, kept), jnp.bfloat16),
        in_specs=[vmem] * (1 + len(raws)),
        out_specs=vmem,
        compiler_params=params,
    )(matrix, *raws)

    near = swap_row(block, 2)
    side = swap_row(block, 1)
    across = swap_row(block, 3)
    out = fisher_part(own_rows, [(0, block), (4, swap_col(block))], None)
    near, out = lax.optimization_barrier((near, out))
    out = fisher_part(own_rows, [(2, near), (1, side), (6, swap_col(near))], out)
    across, out = lax.optimization_barrier((across, out))
    late = [(5, swap_col(side)), (3, across), (7, swap_col(across))]
    out = fisher_part(own_rows, late, out)
    return out.T


def solution(mesh):
    placed = (P(("subj", "row", "col"), None), P(), P(), P("subj"), P("subj"))
    return jax.shard_map(
        body, mesh=mesh, in_specs=placed, out_specs=P("subj", ("row", "col")), check_vma=False
    )
```

```python
import functools

import jax
import jax.numpy as jnp
import numpy as np
from jax import lax
from jax.experimental import pallas as pl
from jax.experimental.pallas import tpu as pltpu
from jax.sharding import PartitionSpec as P

B = 4096
LANES = 128
EPSILON = 1e-06
CLIP_LIMIT = 0.999
HALF_LN2 = 0.34657359027997264
GROUP = 8
AXES = ("row", "col")


def round_up(value, unit):
    return (value + unit - 1) // unit * unit


def band_place(device):
    row, col = device // 2, device % 2
    return col * 4 + row % 4


def shift_band(start_ref, series_ref, band_ref):
    total = series_ref.shape[1]
    start = start_ref[0]
    base = pl.multiple_of(jnp.minimum(start // LANES * LANES, total - B - LANES), LANES)
    rest = start - base
    shift = lax.rem(LANES - rest, LANES)
    lane = lax.broadcasted_iota(jnp.int32, (8, LANES), 1)
    here = lane < LANES - rest
    before = pltpu.roll(series_ref[:, pl.ds(base, LANES)], shift, 1)
    for tile in range(B // LANES):
        after = pltpu.roll(series_ref[:, pl.ds(base + (tile + 1) * LANES, LANES)], shift, 1)
        band_ref[:, tile * LANES : (tile + 1) * LANES] = jnp.where(here, before, after)
        before = after


def own_columns(device, own, own_pad, series_ref):
    columns = series_ref[:, device * own : (device + 1) * own]
    if own_pad > own:
        columns = jnp.concatenate([columns, jnp.zeros((8, own_pad - own), jnp.float32)], 1)
    return columns


def pack_all_kernel(own, start_ref, series_ref, out_ref, band_ref):
    share = B // GROUP
    own_pad = out_ref.shape[2] - share
    shift_band(start_ref, series_ref, band_ref)
    for device in range(out_ref.shape[0]):
        out_ref[device, :, :own_pad] = own_columns(device, own, own_pad, series_ref)
        place = band_place(device)
        out_ref[device, :, own_pad:] = band_ref[:, place * share : (place + 1) * share]


def pack_kernel(own, start_ref, series_ref, straight_ref, cross_ref, band_ref):
    share = B // GROUP
    own_pad = straight_ref.shape[2] - share
    first_core = lax.axis_index("col") == 0
    shift_band(start_ref, series_ref, band_ref)
    for row in range(straight_ref.shape[0]):
        slabs = []
        for device in (2 * row, 2 * row + 1):
            place = band_place(device)
            slabs.append(
                (
                    own_columns(device, own, own_pad, series_ref),
                    band_ref[:, place * share : (place + 1) * share],
                )
            )
        for (low, high), zero, one in zip(((0, own_pad), (own_pad, own_pad + share)), *slabs):
            straight_ref[row, :, low:high] = jnp.where(first_core, zero, one)
            cross_ref[row, :, low:high] = jnp.where(first_core, one, zero)


def merge_kernel(straight_ref, crossed_ref, *out_refs):
    row = lax.axis_index("row")
    for mask, out_ref in enumerate(out_refs):
        out_ref[:8] = straight_ref[row ^ mask]
        out_ref[8:] = crossed_ref[row ^ mask]


def filter_matrix(kept, frames, turn, taps_ref, count_ref, kept_ref):
    n_taps = taps_ref.shape[0]
    reach = n_taps // 2
    shape = (kept, LANES)
    place = lax.broadcasted_iota(jnp.int32, shape, 0)

    def skip(block, carry):
        frame, seen = carry
        seen = seen + kept_ref[block]
        return frame + jnp.where(place >= seen, 8 - kept_ref[block], 0), seen

    frame, _ = lax.fori_loop(0, frames // 8, skip, (place, jnp.int32(0)), unroll=frames <= 128)
    reach_used = count_ref[0]
    tap_sum = jnp.float32(0)
    tap_number = jnp.float32(0)
    for tap in range(n_taps):
        used = abs(tap - reach) <= reach_used
        tap_sum = tap_sum + jnp.where(used, taps_ref[tap], 0.0)
        tap_number = tap_number + jnp.where(used, 1.0, 0.0)
    centre = jnp.full(shape, tap_sum, jnp.float32) / jnp.full(shape, tap_number, jnp.float32)
    pieces = []
    for tile in range(frames // LANES):
        offset = ((lax.broadcasted_iota(jnp.int32, shape, 1) + tile * LANES) ^ turn) - frame
        value = jnp.zeros(shape, jnp.float32)
        for tap in range(n_taps):
            value = jnp.where(offset == tap - reach, taps_ref[tap], value)
        pieces.append(jnp.where(jnp.abs(offset) <= reach_used, value - centre, 0.0))
    return pieces[0] if len(pieces) == 1 else jnp.concatenate(pieces, 1)


def matrix_kernel(relative, taps_ref, count_ref, kept_ref, out_ref):
    kept, frames = out_ref.shape
    turn = 8 * (2 * lax.axis_index("row") + lax.axis_index("col")) if relative else 0
    out_ref[...] = filter_matrix(kept, frames, turn, taps_ref, count_ref, kept_ref)


def scaled_columns(matrix, raw):
    centered = jnp.dot(
        matrix, raw, precision=lax.Precision.HIGHEST, preferred_element_type=jnp.float32
    )
    spread = jnp.sum(centered * centered, axis=0, keepdims=True)
    return centered * lax.rsqrt(spread + EPSILON)


def scale_band_kernel(masks, first, matrix_ref, *refs):
    *raw_refs, band_ref = refs
    raw = jnp.concatenate([raw_refs[i][:, first:] for i in np.argsort(masks)], 0)
    band_ref[...] = scaled_columns(matrix_ref[...], raw).astype(jnp.bfloat16)


def scale_own_kernel(masks, end, matrix_ref, *refs):
    *raw_refs, own_ref = refs
    raw = jnp.concatenate([raw_refs[i][:, :end] for i in np.argsort(masks)], 0)
    scaled = scaled_columns(matrix_ref[...], raw)
    own_ref[...] = scaled.T[: own_ref.shape[0]].astype(jnp.bfloat16)


def fisher_kernel(flips, own_ref, *refs):
    pieces = refs[: len(flips)]
    out_ref, made_ref, sems = refs[-3:]
    share = pieces[0].shape[1]
    half = share // 2
    place = lax.axis_index("col") * 4 + lax.axis_index("row") % 4
    copies = []
    for at, (flip, piece_ref) in enumerate(zip(flips, pieces)):
        for low in (0, half):
            correlation = jnp.dot(
                own_ref[...], piece_ref[:, low : low + half], preferred_element_type=jnp.float32
            )
            c = jnp.clip(correlation, -CLIP_LIMIT, CLIP_LIMIT)
            z_value = HALF_LN2 * (jnp.log2(1.0 + c) - jnp.log2(1.0 - c))
            made_ref[:, at * share + low : at * share + low + half] = z_value.astype(jnp.bfloat16)
        where = pl.multiple_of((place ^ flip) * share, share)
        copy = pltpu.make_async_copy(
            made_ref.at[:, at * share : (at + 1) * share],
            out_ref.at[:, pl.ds(where, share)],
            sems.at[at],
        )
        copy.start()
        copies.append(copy)
    for copy in copies:
        copy.wait()


def fisher_part(own_rows, pieces, out):
    flips = [flip for flip, _ in pieces]
    arrays = [array for _, array in pieces]
    own = own_rows.shape[0]
    vmem = pl.BlockSpec(memory_space=pltpu.VMEM)
    specs = [vmem] * (1 + len(arrays))
    args = [own_rows, *arrays]
    aliases = {}
    if out is not None:
        specs.append(pl.BlockSpec(memory_space=pltpu.HBM))
        aliases = {len(args): 0}
        args.append(out)
    return pl.pallas_call(
        functools.partial(fisher_kernel, flips),
        out_shape=jax.ShapeDtypeStruct((own, B), jnp.bfloat16),
        in_specs=specs,
        out_specs=pl.BlockSpec(memory_space=pltpu.HBM),
        scratch_shapes=[
            pltpu.VMEM((own, len(arrays) * arrays[0].shape[1]), jnp.bfloat16),
            pltpu.SemaphoreType.DMA((len(arrays),)),
        ],
        input_output_aliases=aliases,
        compiler_params=pltpu.CompilerParams(vmem_limit_bytes=48 << 20),
    )(*args)


def body(series, tap_values, tap_count, kept_frames, band_start):
    n_row = lax.axis_size("row")
    n_dev = n_row * lax.axis_size("col")
    frames = 8 * n_dev
    kept = frames * 3 // 4
    total = series.shape[1]
    own = total // n_dev
    own_pad = round_up(own, LANES)
    share = B // GROUP
    smem = pl.BlockSpec(memory_space=pltpu.SMEM)
    vmem = pl.BlockSpec(memory_space=pltpu.VMEM)
    params = pltpu.CompilerParams(vmem_limit_bytes=24 << 20)
    width = own_pad + share

    def swap_row(x, bits):
        return lax.ppermute(x, "row", [(i, i ^ bits) for i in range(n_row)])

    def swap_col(x):
        return lax.ppermute(x, "col", [(0, 1), (1, 0)])

    relative = n_row <= 8
    matrix = pl.pallas_call(
        functools.partial(matrix_kernel, relative),
        out_shape=jax.ShapeDtypeStruct((kept, frames), jnp.float32),
        in_specs=[smem, smem, smem],
        out_specs=vmem,
        compiler_params=params,
    )(tap_values, tap_count, kept_frames)
    if relative:
        slabs = jax.ShapeDtypeStruct((n_row, 8, width), jnp.float32)
        straight, cross = pl.pallas_call(
            functools.partial(pack_kernel, own),
            out_shape=(slabs, slabs),
            in_specs=[smem, vmem],
            out_specs=(vmem, vmem),
            scratch_shapes=[pltpu.VMEM((8, B), jnp.float32)],
            compiler_params=params,
        )(band_start, series)
        raws = list(pl.pallas_call(
            merge_kernel,
            out_shape=[jax.ShapeDtypeStruct((16, width), jnp.float32)] * n_row,
            in_specs=[vmem, vmem],
            out_specs=[vmem] * n_row,
            compiler_params=params,
        )(straight, swap_col(cross)))
        arrived = [raws[0]]
        for mask in range(1, n_row):
            if mask == n_row // 2 - 1:
                raws[mask], *arrived = lax.optimization_barrier((raws[mask], *arrived))
            arrived.append(swap_row(raws[mask], mask))
        masks = [*range(1, n_row), 0]
        raws = [arrived[mask] for mask in masks]
    else:
        packed = pl.pallas_call(
            functools.partial(pack_all_kernel, own),
            out_shape=jax.ShapeDtypeStruct((n_dev, 8, width), jnp.float32),
            in_specs=[smem, vmem],
            out_specs=vmem,
            scratch_shapes=[pltpu.VMEM((8, B), jnp.float32)],
            compiler_params=params,
        )(band_start, series)
        masks = [0]
        raws = [lax.all_to_all(packed, AXES, 0, 0, tiled=True).reshape(frames, width)]
    block = pl.pallas_call(
        functools.partial(scale_band_kernel, masks, own_pad),
        out_shape=jax.ShapeDtypeStruct((kept, share), jnp.bfloat16),
        in_specs=[vmem] * (1 + len(raws)),
        out_specs=vmem,
        compiler_params=params,
    )(matrix, *raws)
    own_rows = pl.pallas_call(
        functools.partial(scale_own_kernel, masks, own_pad),
        out_shape=jax.ShapeDtypeStruct((own, kept), jnp.bfloat16),
        in_specs=[vmem] * (1 + len(raws)),
        out_specs=vmem,
        compiler_params=params,
    )(matrix, *raws)

    near = swap_row(block, 2)
    side = swap_row(block, 1)
    across = swap_row(block, 3)
    early = [(0, block), (4, swap_col(block)), (2, near)]
    out = fisher_part(own_rows, early, None)
    side, across, out = lax.optimization_barrier((side, across, out))
    late = [(6, swap_col(near)), (1, side), (3, across), (5, swap_col(side)), (7, swap_col(across))]
    out = fisher_part(own_rows, late, out)
    return out.T


def solution(mesh):
    placed = (P(("subj", "row", "col"), None), P(), P(), P("subj"), P("subj"))
    return jax.shard_map(
        body, mesh=mesh, in_specs=placed, out_specs=P("subj", ("row", "col")), check_vma=False
    )
```

```python
import functools

import jax
import jax.numpy as jnp
from jax import lax
from jax.experimental import pallas as pl
from jax.experimental.pallas import tpu as pltpu
from jax.sharding import PartitionSpec as P

B = 4096
LANES = 128
EPSILON = 1e-06
CLIP_LIMIT = 0.999
HALF_LN2 = 0.34657359027997264
GROUP = 8
AXES = ("row", "col")


def round_up(value, unit):
    return (value + unit - 1) // unit * unit


def band_place(device):
    row, col = device // 2, device % 2
    return col * 4 + row % 4


def shift_band(start_ref, series_ref, band_ref):
    total = series_ref.shape[1]
    start = jnp.max(start_ref[...])
    base = pl.multiple_of(jnp.minimum(start // LANES * LANES, total - B - LANES), LANES)
    rest = start - base
    shift = lax.rem(LANES - rest, LANES)
    lane = lax.broadcasted_iota(jnp.int32, (8, LANES), 1)
    here = lane < LANES - rest
    before = pltpu.roll(series_ref[:, pl.ds(base, LANES)], shift, 1)
    for tile in range(B // LANES):
        after = pltpu.roll(series_ref[:, pl.ds(base + (tile + 1) * LANES, LANES)], shift, 1)
        band_ref[:, tile * LANES : (tile + 1) * LANES] = jnp.where(here, before, after)
        before = after


def own_columns(device, own, own_pad, series_ref):
    columns = series_ref[:, device * own : (device + 1) * own]
    if own_pad > own:
        columns = jnp.concatenate([columns, jnp.zeros((8, own_pad - own), jnp.float32)], 1)
    return columns


def pack_all_kernel(own, start_ref, series_ref, out_ref, band_ref):
    share = B // GROUP
    own_pad = out_ref.shape[2] - share
    shift_band(start_ref, series_ref, band_ref)
    for device in range(out_ref.shape[0]):
        out_ref[device, :, :own_pad] = own_columns(device, own, own_pad, series_ref)
        place = band_place(device)
        out_ref[device, :, own_pad:] = band_ref[:, place * share : (place + 1) * share]


def pack_kernel(own, start_ref, series_ref, straight_ref, cross_ref, band_ref):
    share = B // GROUP
    own_pad = straight_ref.shape[2] - share
    first_core = lax.axis_index("col") == 0
    shift_band(start_ref, series_ref, band_ref)
    for row in range(straight_ref.shape[0]):
        slabs = []
        for device in (2 * row, 2 * row + 1):
            place = band_place(device)
            slabs.append(
                (
                    own_columns(device, own, own_pad, series_ref),
                    band_ref[:, place * share : (place + 1) * share],
                )
            )
        for (low, high), zero, one in zip(((0, own_pad), (own_pad, own_pad + share)), *slabs):
            straight_ref[row, :, low:high] = jnp.where(first_core, zero, one)
            cross_ref[row, :, low:high] = jnp.where(first_core, one, zero)


def merge_kernel(straight_ref, crossed_ref, own_ref, y_ref, z_ref, *far_refs):
    row = lax.axis_index("row")
    spots = [(own_ref, 0), (y_ref, 0), (z_ref, 0), (z_ref, 16), *((ref, 0) for ref in far_refs)]
    for mask, (out_ref, at) in enumerate(spots):
        out_ref[at : at + 8] = straight_ref[row ^ mask]
        out_ref[at + 8 : at + 16] = crossed_ref[row ^ mask]


def relay_kernel(y_ref, z_ref, out_ref):
    out_ref[:16] = y_ref[:16]
    out_ref[16:] = z_ref[16:]


def frames_of(refs, low, high):
    if len(refs) == 1:
        return refs[0][:, low:high]
    *far_refs, y_ref, z_ref, own_ref = refs
    near = [own_ref[...], y_ref[:16], z_ref[:16], y_ref[16:]]
    return jnp.concatenate([part[:, low:high] for part in near + [ref[...] for ref in far_refs]], 0)


def filter_matrix(kept, frames, turn, taps_ref, count_ref, kept_ref):
    n_taps = taps_ref.shape[0]
    reach = n_taps // 2
    shape = (kept, LANES)
    place = lax.broadcasted_iota(jnp.int32, shape, 0)

    def skip(block, carry):
        frame, seen = carry
        seen = seen + kept_ref[block]
        return frame + jnp.where(place >= seen, 8 - kept_ref[block], 0), seen

    frame, _ = lax.fori_loop(0, frames // 8, skip, (place, jnp.int32(0)), unroll=frames <= 128)
    reach_used = count_ref[0]
    tap_sum = jnp.float32(0)
    tap_number = jnp.float32(0)
    for tap in range(n_taps):
        used = abs(tap - reach) <= reach_used
        tap_sum = tap_sum + jnp.where(used, taps_ref[tap], 0.0)
        tap_number = tap_number + jnp.where(used, 1.0, 0.0)
    centre = jnp.full(shape, tap_sum, jnp.float32) / jnp.full(shape, tap_number, jnp.float32)
    pieces = []
    for tile in range(frames // LANES):
        offset = ((lax.broadcasted_iota(jnp.int32, shape, 1) + tile * LANES) ^ turn) - frame
        value = jnp.zeros(shape, jnp.float32)
        for tap in range(n_taps):
            value = jnp.where(offset == tap - reach, taps_ref[tap], value)
        pieces.append(jnp.where(jnp.abs(offset) <= reach_used, value - centre, 0.0))
    return pieces[0] if len(pieces) == 1 else jnp.concatenate(pieces, 1)


def matrix_kernel(relative, taps_ref, count_ref, kept_ref, out_ref):
    kept, frames = out_ref.shape
    turn = 8 * (2 * lax.axis_index("row") + lax.axis_index("col")) if relative else 0
    out_ref[...] = filter_matrix(kept, frames, turn, taps_ref, count_ref, kept_ref)


def scaled_columns(matrix, raw):
    centered = jnp.dot(
        matrix, raw, precision=lax.Precision.HIGHEST, preferred_element_type=jnp.float32
    )
    spread = jnp.sum(centered * centered, axis=0, keepdims=True)
    return centered * lax.rsqrt(spread + EPSILON)


def scale_band_kernel(first, matrix_ref, *refs):
    *raw_refs, band_ref = refs
    raw = frames_of(raw_refs, first, first + band_ref.shape[1])
    band_ref[...] = scaled_columns(matrix_ref[...], raw).astype(jnp.bfloat16)


def scale_own_kernel(end, matrix_ref, *refs):
    *raw_refs, own_ref = refs
    raw = frames_of(raw_refs, 0, end)
    scaled = scaled_columns(matrix_ref[...], raw)
    own_ref[...] = scaled.T[: own_ref.shape[0]].astype(jnp.bfloat16)


def fisher_kernel(flips, own_ref, *refs):
    pieces = refs[: len(flips)]
    out_ref, made_ref, sems = refs[-3:]
    share = pieces[0].shape[1]
    half = share // 2
    place = lax.axis_index("col") * 4 + lax.axis_index("row") % 4
    copies = []
    for at, (flip, piece_ref) in enumerate(zip(flips, pieces)):
        for low in (0, half):
            correlation = jnp.dot(
                own_ref[...], piece_ref[:, low : low + half], preferred_element_type=jnp.float32
            )
            c = jnp.clip(correlation, -CLIP_LIMIT, CLIP_LIMIT)
            z_value = HALF_LN2 * (jnp.log2(1.0 + c) - jnp.log2(1.0 - c))
            made_ref[:, at * share + low : at * share + low + half] = z_value.astype(jnp.bfloat16)
        where = pl.multiple_of((place ^ flip) * share, share)
        copy = pltpu.make_async_copy(
            made_ref.at[:, at * share : (at + 1) * share],
            out_ref.at[:, pl.ds(where, share)],
            sems.at[at],
        )
        copy.start()
        copies.append(copy)
    for copy in copies:
        copy.wait()


def fisher_part(own_rows, pieces, out):
    flips = [flip for flip, _ in pieces]
    arrays = [array for _, array in pieces]
    own = own_rows.shape[0]
    vmem = pl.BlockSpec(memory_space=pltpu.VMEM)
    specs = [vmem] * (1 + len(arrays))
    args = [own_rows, *arrays]
    aliases = {}
    if out is not None:
        specs.append(pl.BlockSpec(memory_space=pltpu.HBM))
        aliases = {len(args): 0}
        args.append(out)
    return pl.pallas_call(
        functools.partial(fisher_kernel, flips),
        out_shape=jax.ShapeDtypeStruct((own, B), jnp.bfloat16),
        in_specs=specs,
        out_specs=pl.BlockSpec(memory_space=pltpu.HBM),
        scratch_shapes=[
            pltpu.VMEM((own, len(arrays) * arrays[0].shape[1]), jnp.bfloat16),
            pltpu.SemaphoreType.DMA((len(arrays),)),
        ],
        input_output_aliases=aliases,
        compiler_params=pltpu.CompilerParams(vmem_limit_bytes=48 << 20),
    )(*args)


def body(series, tap_values, tap_count, kept_frames, band_start):
    n_row = lax.axis_size("row")
    n_dev = n_row * lax.axis_size("col")
    frames = 8 * n_dev
    kept = frames * 3 // 4
    total = series.shape[1]
    own = total // n_dev
    own_pad = round_up(own, LANES)
    share = B // GROUP
    smem = pl.BlockSpec(memory_space=pltpu.SMEM)
    vmem = pl.BlockSpec(memory_space=pltpu.VMEM)
    params = pltpu.CompilerParams(vmem_limit_bytes=24 << 20)
    width = own_pad + share

    def swap_row(x, bits):
        return lax.ppermute(x, "row", [(i, i ^ bits) for i in range(n_row)])

    def swap_col(x):
        return lax.ppermute(x, "col", [(0, 1), (1, 0)])

    relative = n_row == 8
    matrix = pl.pallas_call(
        functools.partial(matrix_kernel, relative),
        out_shape=jax.ShapeDtypeStruct((kept, frames), jnp.float32),
        in_specs=[smem, smem, smem],
        out_specs=vmem,
        cost_estimate=pl.CostEstimate(flops=10**10, transcendentals=0, bytes_accessed=10**8),
        compiler_params=params,
    )(tap_values, tap_count, kept_frames)
    if relative:
        slabs = jax.ShapeDtypeStruct((n_row, 8, width), jnp.float32)
        straight, cross = pl.pallas_call(
            functools.partial(pack_kernel, own),
            out_shape=(slabs, slabs),
            in_specs=[vmem, vmem],
            out_specs=(vmem, vmem),
            scratch_shapes=[pltpu.VMEM((8, B), jnp.float32)],
            compiler_params=params,
        )(band_start.reshape(1, 1), series)
        one, two = (jax.ShapeDtypeStruct((16 * count, width), jnp.float32) for count in (1, 2))
        own_raw, y_raw, z_raw, *far_raws = pl.pallas_call(
            merge_kernel,
            out_shape=[one, two, two] + [one] * (n_row - 4),
            in_specs=[vmem, vmem],
            out_specs=[vmem] * (n_row - 1),
            compiler_params=params,
        )(straight, swap_col(cross))
        raws = [swap_row(raw, mask) for mask, raw in enumerate(far_raws, 4)]
        z_raw = swap_row(z_raw, 2)
        y_raw = pl.pallas_call(
            relay_kernel,
            out_shape=two,
            in_specs=[vmem, vmem],
            out_specs=vmem,
            input_output_aliases={0: 0},
            compiler_params=params,
        )(y_raw, z_raw)
        raws += [swap_row(y_raw, 1), z_raw, own_raw]
    else:
        packed = pl.pallas_call(
            functools.partial(pack_all_kernel, own),
            out_shape=jax.ShapeDtypeStruct((n_dev, 8, width), jnp.float32),
            in_specs=[vmem, vmem],
            out_specs=vmem,
            scratch_shapes=[pltpu.VMEM((8, B), jnp.float32)],
            compiler_params=params,
        )(band_start.reshape(1, 1), series)
        raws = [lax.all_to_all(packed, AXES, 0, 0, tiled=True).reshape(frames, width)]
    block = pl.pallas_call(
        functools.partial(scale_band_kernel, own_pad),
        out_shape=jax.ShapeDtypeStruct((kept, share), jnp.bfloat16),
        in_specs=[vmem] * (1 + len(raws)),
        out_specs=vmem,
        compiler_params=params,
    )(matrix, *raws)
    own_rows = pl.pallas_call(
        functools.partial(scale_own_kernel, own_pad),
        out_shape=jax.ShapeDtypeStruct((own, kept), jnp.bfloat16),
        in_specs=[vmem] * (1 + len(raws)),
        out_specs=vmem,
        compiler_params=params,
    )(matrix, *raws)

    across = swap_row(block, 3)
    near = swap_row(block, 2)
    side = swap_row(block, 1)
    out = fisher_part(own_rows, [(0, block), (4, swap_col(block))], None)
    across, out = lax.optimization_barrier((across, out))
    late = [(2, near), (1, side), (3, across)]
    late += [(6, swap_col(near)), (5, swap_col(side)), (7, swap_col(across))]
    out = fisher_part(own_rows, late, out)
    return out.T


def solution(mesh):
    placed = (P(("subj", "row", "col"), None), P(), P(), P("subj"), P("subj"))
    return jax.shard_map(
        body, mesh=mesh, in_specs=placed, out_specs=P("subj", ("row", "col")), check_vma=False
    )
```

```python
import functools

import jax
import jax.numpy as jnp
from jax import lax
from jax.experimental import pallas as pl
from jax.experimental.pallas import tpu as pltpu
from jax.sharding import PartitionSpec as P

B = 4096
LANES = 128
EPSILON = 1e-06
CLIP_LIMIT = 0.999
HALF_LN2 = 0.34657359027997264
GROUP = 8
AXES = ("row", "col")


def round_up(value, unit):
    return (value + unit - 1) // unit * unit


def band_place(device):
    row, col = device // 2, device % 2
    return col * 4 + row % 4


def shift_band(start_ref, series_ref, band_ref):
    total = series_ref.shape[1]
    start = jnp.max(start_ref[...])
    base = pl.multiple_of(jnp.minimum(start // LANES * LANES, total - B - LANES), LANES)
    rest = start - base
    shift = lax.rem(LANES - rest, LANES)
    lane = lax.broadcasted_iota(jnp.int32, (8, LANES), 1)
    here = lane < LANES - rest
    before = pltpu.roll(series_ref[:, pl.ds(base, LANES)], shift, 1)
    for tile in range(B // LANES):
        after = pltpu.roll(series_ref[:, pl.ds(base + (tile + 1) * LANES, LANES)], shift, 1)
        band_ref[:, tile * LANES : (tile + 1) * LANES] = jnp.where(here, before, after)
        before = after


def own_columns(device, own, own_pad, series_ref):
    columns = series_ref[:, device * own : (device + 1) * own]
    if own_pad > own:
        columns = jnp.concatenate([columns, jnp.zeros((8, own_pad - own), jnp.float32)], 1)
    return columns


def pack_all_kernel(own, start_ref, series_ref, out_ref, band_ref):
    share = B // GROUP
    own_pad = out_ref.shape[2] - share
    shift_band(start_ref, series_ref, band_ref)
    for device in range(out_ref.shape[0]):
        out_ref[device, :, :own_pad] = own_columns(device, own, own_pad, series_ref)
        place = band_place(device)
        out_ref[device, :, own_pad:] = band_ref[:, place * share : (place + 1) * share]


def pack_kernel(own, start_ref, series_ref, straight_ref, cross_ref, band_ref):
    share = B // GROUP
    own_pad = straight_ref.shape[2] - share
    first_core = lax.axis_index("col") == 0
    shift_band(start_ref, series_ref, band_ref)
    for row in range(straight_ref.shape[0]):
        slabs = []
        for device in (2 * row, 2 * row + 1):
            place = band_place(device)
            slabs.append(
                (
                    own_columns(device, own, own_pad, series_ref),
                    band_ref[:, place * share : (place + 1) * share],
                )
            )
        for (low, high), zero, one in zip(((0, own_pad), (own_pad, own_pad + share)), *slabs):
            straight_ref[row, :, low:high] = jnp.where(first_core, zero, one)
            cross_ref[row, :, low:high] = jnp.where(first_core, one, zero)


def merge_kernel(straight_ref, crossed_ref, _, own_ref, y_ref, z_ref, *far_refs):
    row = lax.axis_index("row")
    spots = [(own_ref, 0), (y_ref, 0), (z_ref, 0), (z_ref, 16), *((ref, 0) for ref in far_refs)]
    for mask, (out_ref, at) in enumerate(spots):
        out_ref[at : at + 8] = straight_ref[row ^ mask]
        out_ref[at + 8 : at + 16] = crossed_ref[row ^ mask]


def relay_kernel(y_ref, z_ref, out_ref):
    out_ref[:16] = y_ref[:16]
    out_ref[16:] = z_ref[16:]


def frames_of(refs, low, high):
    if len(refs) == 1:
        return refs[0][:, low:high]
    *far_refs, y_ref, z_ref, own_ref = refs
    near = [own_ref[...], y_ref[:16], z_ref[:16], y_ref[16:]]
    return jnp.concatenate([part[:, low:high] for part in near + [ref[...] for ref in far_refs]], 0)


def filter_matrix(kept, frames, turn, taps_ref, count_ref, kept_ref):
    n_taps = taps_ref.shape[0]
    reach = n_taps // 2
    shape = (kept, LANES)
    place = lax.broadcasted_iota(jnp.int32, shape, 0)

    def skip(block, carry):
        frame, seen = carry
        seen = seen + kept_ref[block]
        return frame + jnp.where(place >= seen, 8 - kept_ref[block], 0), seen

    frame, _ = lax.fori_loop(0, frames // 8, skip, (place, jnp.int32(0)), unroll=frames <= 128)
    reach_used = count_ref[0]
    tap_sum = jnp.float32(0)
    tap_number = jnp.float32(0)
    for tap in range(n_taps):
        used = abs(tap - reach) <= reach_used
        tap_sum = tap_sum + jnp.where(used, taps_ref[tap], 0.0)
        tap_number = tap_number + jnp.where(used, 1.0, 0.0)
    centre = jnp.full(shape, tap_sum, jnp.float32) / jnp.full(shape, tap_number, jnp.float32)
    pieces = []
    for tile in range(frames // LANES):
        offset = ((lax.broadcasted_iota(jnp.int32, shape, 1) + tile * LANES) ^ turn) - frame
        value = jnp.zeros(shape, jnp.float32)
        for tap in range(n_taps):
            value = jnp.where(offset == tap - reach, taps_ref[tap], value)
        pieces.append(jnp.where(jnp.abs(offset) <= reach_used, value - centre, 0.0))
    return pieces[0] if len(pieces) == 1 else jnp.concatenate(pieces, 1)


def matrix_kernel(relative, taps_ref, count_ref, kept_ref, out_ref):
    kept, frames = out_ref.shape
    turn = 8 * (2 * lax.axis_index("row") + lax.axis_index("col")) if relative else 0
    out_ref[...] = filter_matrix(kept, frames, turn, taps_ref, count_ref, kept_ref)


def scaled_columns(matrix, raw):
    centered = jnp.dot(
        matrix, raw, precision=lax.Precision.HIGHEST, preferred_element_type=jnp.float32
    )
    spread = jnp.sum(centered * centered, axis=0, keepdims=True)
    return centered * lax.rsqrt(spread + EPSILON)


def scale_band_kernel(first, matrix_ref, *refs):
    *raw_refs, band_ref = refs
    raw = frames_of(raw_refs, first, first + band_ref.shape[1])
    band_ref[...] = scaled_columns(matrix_ref[...], raw).astype(jnp.bfloat16)


def scale_own_kernel(end, matrix_ref, *refs):
    *raw_refs, own_ref = refs
    raw = frames_of(raw_refs, 0, end)
    scaled = scaled_columns(matrix_ref[...], raw)
    own_ref[...] = scaled.T[: own_ref.shape[0]].astype(jnp.bfloat16)


def fisher_kernel(flips, own_ref, *refs):
    pieces = refs[: len(flips)]
    out_ref, made_ref, sems = refs[-3:]
    share = pieces[0].shape[1]
    half = share // 2
    place = lax.axis_index("col") * 4 + lax.axis_index("row") % 4
    copies = []
    for at, (flip, piece_ref) in enumerate(zip(flips, pieces)):
        for low in (0, half):
            correlation = jnp.dot(
                own_ref[...], piece_ref[:, low : low + half], preferred_element_type=jnp.float32
            )
            c = jnp.clip(correlation, -CLIP_LIMIT, CLIP_LIMIT)
            z_value = HALF_LN2 * (jnp.log2(1.0 + c) - jnp.log2(1.0 - c))
            made_ref[:, at * share + low : at * share + low + half] = z_value.astype(jnp.bfloat16)
        where = pl.multiple_of((place ^ flip) * share, share)
        copy = pltpu.make_async_copy(
            made_ref.at[:, at * share : (at + 1) * share],
            out_ref.at[:, pl.ds(where, share)],
            sems.at[at],
        )
        copy.start()
        copies.append(copy)
    for copy in copies:
        copy.wait()


def fisher_part(own_rows, pieces, out):
    flips = [flip for flip, _ in pieces]
    arrays = [array for _, array in pieces]
    own = own_rows.shape[0]
    vmem = pl.BlockSpec(memory_space=pltpu.VMEM)
    specs = [vmem] * (1 + len(arrays))
    args = [own_rows, *arrays]
    aliases = {}
    if out is not None:
        specs.append(pl.BlockSpec(memory_space=pltpu.HBM))
        aliases = {len(args): 0}
        args.append(out)
    return pl.pallas_call(
        functools.partial(fisher_kernel, flips),
        out_shape=jax.ShapeDtypeStruct((own, B), jnp.bfloat16),
        in_specs=specs,
        out_specs=pl.BlockSpec(memory_space=pltpu.HBM),
        scratch_shapes=[
            pltpu.VMEM((own, len(arrays) * arrays[0].shape[1]), jnp.bfloat16),
            pltpu.SemaphoreType.DMA((len(arrays),)),
        ],
        input_output_aliases=aliases,
        compiler_params=pltpu.CompilerParams(vmem_limit_bytes=48 << 20),
    )(*args)


def body(series, tap_values, tap_count, kept_frames, band_start):
    n_row = lax.axis_size("row")
    n_dev = n_row * lax.axis_size("col")
    frames = 8 * n_dev
    kept = frames * 3 // 4
    total = series.shape[1]
    own = total // n_dev
    own_pad = round_up(own, LANES)
    share = B // GROUP
    smem = pl.BlockSpec(memory_space=pltpu.SMEM)
    vmem = pl.BlockSpec(memory_space=pltpu.VMEM)
    params = pltpu.CompilerParams(vmem_limit_bytes=24 << 20)
    width = own_pad + share

    def swap_row(x, bits):
        return lax.ppermute(x, "row", [(i, i ^ bits) for i in range(n_row)])

    def swap_col(x):
        return lax.ppermute(x, "col", [(0, 1), (1, 0)])

    relative = n_row == 8
    matrix = pl.pallas_call(
        functools.partial(matrix_kernel, relative),
        out_shape=jax.ShapeDtypeStruct((kept, frames), jnp.float32),
        in_specs=[smem, smem, smem],
        out_specs=vmem,
        cost_estimate=pl.CostEstimate(flops=10**10, transcendentals=0, bytes_accessed=10**8),
        compiler_params=params,
    )(tap_values, tap_count, kept_frames)
    if relative:
        slabs = jax.ShapeDtypeStruct((n_row, 8, width), jnp.float32)
        straight, cross = pl.pallas_call(
            functools.partial(pack_kernel, own),
            out_shape=(slabs, slabs),
            in_specs=[vmem, vmem],
            out_specs=(vmem, vmem),
            scratch_shapes=[pltpu.VMEM((8, B), jnp.float32)],
            compiler_params=params,
        )(band_start.reshape(1, 1), series)
        one, two = (jax.ShapeDtypeStruct((16 * count, width), jnp.float32) for count in (1, 2))
        own_raw, y_raw, z_raw, *far_raws = pl.pallas_call(
            merge_kernel,
            out_shape=[one, two, two] + [one] * (n_row - 4),
            in_specs=[vmem, vmem, smem],
            out_specs=[vmem] * (n_row - 1),
            compiler_params=params,
        )(straight, swap_col(cross), tap_count)
        raws = [swap_row(raw, mask) for mask, raw in enumerate(far_raws, 4)]
        z_raw = swap_row(z_raw, 2)
        y_raw = pl.pallas_call(
            relay_kernel,
            out_shape=two,
            in_specs=[vmem, vmem],
            out_specs=vmem,
            input_output_aliases={0: 0},
            compiler_params=params,
        )(y_raw, z_raw)
        raws += [swap_row(y_raw, 1), z_raw, own_raw]
    else:
        packed = pl.pallas_call(
            functools.partial(pack_all_kernel, own),
            out_shape=jax.ShapeDtypeStruct((n_dev, 8, width), jnp.float32),
            in_specs=[vmem, vmem],
            out_specs=vmem,
            scratch_shapes=[pltpu.VMEM((8, B), jnp.float32)],
            compiler_params=params,
        )(band_start.reshape(1, 1), series)
        raws = [lax.all_to_all(packed, AXES, 0, 0, tiled=True).reshape(frames, width)]
    block = pl.pallas_call(
        functools.partial(scale_band_kernel, own_pad),
        out_shape=jax.ShapeDtypeStruct((kept, share), jnp.bfloat16),
        in_specs=[vmem] * (1 + len(raws)),
        out_specs=vmem,
        compiler_params=params,
    )(matrix, *raws)
    own_rows = pl.pallas_call(
        functools.partial(scale_own_kernel, own_pad),
        out_shape=jax.ShapeDtypeStruct((own, kept), jnp.bfloat16),
        in_specs=[vmem] * (1 + len(raws)),
        out_specs=vmem,
        compiler_params=params,
    )(matrix, *raws)

    across = swap_row(block, 3)
    near = swap_row(block, 2)
    side = swap_row(block, 1)
    out = fisher_part(own_rows, [(0, block), (4, swap_col(block))], None)
    across, out = lax.optimization_barrier((across, out))
    late = [(2, near), (1, side), (3, across)]
    late += [(6, swap_col(near)), (5, swap_col(side)), (7, swap_col(across))]
    out = fisher_part(own_rows, late, out)
    return out.T


def solution(mesh):
    placed = (P(("subj", "row", "col"), None), P(), P(), P("subj"), P("subj"))
    return jax.shard_map(
        body, mesh=mesh, in_specs=placed, out_specs=P("subj", ("row", "col")), check_vma=False
    )
```

```python
import functools

import jax
import jax.numpy as jnp
from jax import lax
from jax.experimental import pallas as pl
from jax.experimental.pallas import tpu as pltpu
from jax.sharding import PartitionSpec as P

B = 4096
LANES = 128
EPSILON = 1e-06
CLIP_LIMIT = 0.999
HALF_LN2 = 0.34657359027997264
GROUP = 8
AXES = ("row", "col")


def round_up(value, unit):
    return (value + unit - 1) // unit * unit


def band_place(device):
    row, col = device // 2, device % 2
    return col * 4 + row % 4


def shift_band(start_ref, series_ref, band_ref):
    total = series_ref.shape[1]
    start = jnp.max(start_ref[...])
    base = pl.multiple_of(jnp.minimum(start // LANES * LANES, total - B - LANES), LANES)
    rest = start - base
    shift = lax.rem(LANES - rest, LANES)
    lane = lax.broadcasted_iota(jnp.int32, (8, LANES), 1)
    here = lane < LANES - rest
    before = pltpu.roll(series_ref[:, pl.ds(base, LANES)], shift, 1)
    for tile in range(B // LANES):
        after = pltpu.roll(series_ref[:, pl.ds(base + (tile + 1) * LANES, LANES)], shift, 1)
        band_ref[:, tile * LANES : (tile + 1) * LANES] = jnp.where(here, before, after)
        before = after


def own_columns(device, own, own_pad, series_ref):
    columns = series_ref[:, device * own : (device + 1) * own]
    if own_pad > own:
        columns = jnp.concatenate([columns, jnp.zeros((8, own_pad - own), jnp.float32)], 1)
    return columns


def pack_all_kernel(own, start_ref, series_ref, out_ref, band_ref):
    share = B // GROUP
    own_pad = out_ref.shape[2] - share
    shift_band(start_ref, series_ref, band_ref)
    for device in range(out_ref.shape[0]):
        out_ref[device, :, :own_pad] = own_columns(device, own, own_pad, series_ref)
        place = band_place(device)
        out_ref[device, :, own_pad:] = band_ref[:, place * share : (place + 1) * share]


def pack_kernel(own, start_ref, series_ref, straight_ref, cross_ref, band_ref):
    share = B // GROUP
    own_pad = straight_ref.shape[2] - share
    first_core = lax.axis_index("col") == 0
    shift_band(start_ref, series_ref, band_ref)
    for row in range(straight_ref.shape[0]):
        slabs = []
        for device in (2 * row, 2 * row + 1):
            place = band_place(device)
            slabs.append(
                (
                    own_columns(device, own, own_pad, series_ref),
                    band_ref[:, place * share : (place + 1) * share],
                )
            )
        for (low, high), zero, one in zip(((0, own_pad), (own_pad, own_pad + share)), *slabs):
            straight_ref[row, :, low:high] = jnp.where(first_core, zero, one)
            cross_ref[row, :, low:high] = jnp.where(first_core, one, zero)


def merge_kernel(straight_ref, crossed_ref, _, own_ref, y_ref, z_ref, *far_refs):
    row = lax.axis_index("row")
    spots = [(own_ref, 0), (y_ref, 0), (z_ref, 0), (z_ref, 16), *((ref, 0) for ref in far_refs)]
    for mask, (out_ref, at) in enumerate(spots):
        out_ref[at : at + 8] = straight_ref[row ^ mask]
        out_ref[at + 8 : at + 16] = crossed_ref[row ^ mask]


def relay_kernel(y_ref, z_ref, out_ref):
    out_ref[:16] = y_ref[:16]
    out_ref[16:] = z_ref[16:]


def frames_of(refs, low, high):
    if len(refs) == 1:
        return refs[0][:, low:high]
    *far_refs, y_ref, z_ref, own_ref = refs
    near = [own_ref[...], y_ref[:16], z_ref[:16], y_ref[16:]]
    return jnp.concatenate([part[:, low:high] for part in near + [ref[...] for ref in far_refs]], 0)


def filter_matrix(kept, frames, turn, taps_ref, count_ref, kept_ref):
    n_taps = taps_ref.shape[0]
    reach = n_taps // 2
    shape = (kept, LANES)
    place = lax.broadcasted_iota(jnp.int32, shape, 0)

    def skip(block, carry):
        frame, seen = carry
        seen = seen + kept_ref[block]
        return frame + jnp.where(place >= seen, 8 - kept_ref[block], 0), seen

    frame, _ = lax.fori_loop(0, frames // 8, skip, (place, jnp.int32(0)), unroll=frames <= 128)
    reach_used = count_ref[0]
    tap_sum = jnp.float32(0)
    tap_number = jnp.float32(0)
    for tap in range(n_taps):
        used = abs(tap - reach) <= reach_used
        tap_sum = tap_sum + jnp.where(used, taps_ref[tap], 0.0)
        tap_number = tap_number + jnp.where(used, 1.0, 0.0)
    centre = jnp.full(shape, tap_sum, jnp.float32) / jnp.full(shape, tap_number, jnp.float32)
    pieces = []
    for tile in range(frames // LANES):
        offset = ((lax.broadcasted_iota(jnp.int32, shape, 1) + tile * LANES) ^ turn) - frame
        value = jnp.zeros(shape, jnp.float32)
        for tap in range(n_taps):
            value = jnp.where(offset == tap - reach, taps_ref[tap], value)
        pieces.append(jnp.where(jnp.abs(offset) <= reach_used, value - centre, 0.0))
    return pieces[0] if len(pieces) == 1 else jnp.concatenate(pieces, 1)


def matrix_kernel(relative, taps_ref, count_ref, kept_ref, out_ref):
    kept, frames = out_ref.shape
    turn = 8 * (2 * lax.axis_index("row") + lax.axis_index("col")) if relative else 0
    out_ref[...] = filter_matrix(kept, frames, turn, taps_ref, count_ref, kept_ref)


def scaled_columns(matrix, raw):
    centered = jnp.dot(
        matrix, raw, precision=lax.Precision.HIGHEST, preferred_element_type=jnp.float32
    )
    spread = jnp.sum(centered * centered, axis=0, keepdims=True)
    return centered * lax.rsqrt(spread + EPSILON)


def scale_band_kernel(first, matrix_ref, *refs):
    *raw_refs, band_ref = refs
    raw = frames_of(raw_refs, first, first + band_ref.shape[1])
    band_ref[...] = scaled_columns(matrix_ref[...], raw).astype(jnp.bfloat16)


def scale_own_kernel(end, matrix_ref, *refs):
    *raw_refs, own_ref = refs
    raw = frames_of(raw_refs, 0, end)
    scaled = scaled_columns(matrix_ref[...], raw)
    own_ref[...] = scaled.T[: own_ref.shape[0]].astype(jnp.bfloat16)


def fisher_kernel(flips, own_ref, *refs):
    pieces = refs[: len(flips)]
    out_ref, made_ref, sems = refs[-3:]
    share = pieces[0].shape[1]
    half = share // 2
    place = lax.axis_index("col") * 4 + lax.axis_index("row") % 4
    copies = []
    for at, (flip, piece_ref) in enumerate(zip(flips, pieces)):
        for low in (0, half):
            correlation = jnp.dot(
                own_ref[...], piece_ref[:, low : low + half], preferred_element_type=jnp.float32
            )
            c = jnp.clip(correlation, -CLIP_LIMIT, CLIP_LIMIT)
            z_value = HALF_LN2 * (jnp.log2(1.0 + c) - jnp.log2(1.0 - c))
            made_ref[:, at * share + low : at * share + low + half] = z_value.astype(jnp.bfloat16)
        where = pl.multiple_of((place ^ flip) * share, share)
        copy = pltpu.make_async_copy(
            made_ref.at[:, at * share : (at + 1) * share],
            out_ref.at[:, pl.ds(where, share)],
            sems.at[at],
        )
        copy.start()
        copies.append(copy)
    for copy in copies:
        copy.wait()


def fisher_part(own_rows, pieces, out):
    flips = [flip for flip, _ in pieces]
    arrays = [array for _, array in pieces]
    own = own_rows.shape[0]
    vmem = pl.BlockSpec(memory_space=pltpu.VMEM)
    specs = [vmem] * (1 + len(arrays))
    args = [own_rows, *arrays]
    aliases = {}
    if out is not None:
        specs.append(pl.BlockSpec(memory_space=pltpu.HBM))
        aliases = {len(args): 0}
        args.append(out)
    return pl.pallas_call(
        functools.partial(fisher_kernel, flips),
        out_shape=jax.ShapeDtypeStruct((own, B), jnp.bfloat16),
        in_specs=specs,
        out_specs=pl.BlockSpec(memory_space=pltpu.HBM),
        scratch_shapes=[
            pltpu.VMEM((own, len(arrays) * arrays[0].shape[1]), jnp.bfloat16),
            pltpu.SemaphoreType.DMA((len(arrays),)),
        ],
        input_output_aliases=aliases,
        compiler_params=pltpu.CompilerParams(vmem_limit_bytes=48 << 20),
    )(*args)


def body(series, tap_values, tap_count, kept_frames, band_start):
    n_row = lax.axis_size("row")
    n_dev = n_row * lax.axis_size("col")
    frames = 8 * n_dev
    kept = frames * 3 // 4
    total = series.shape[1]
    own = total // n_dev
    own_pad = round_up(own, LANES)
    share = B // GROUP
    smem = pl.BlockSpec(memory_space=pltpu.SMEM)
    vmem = pl.BlockSpec(memory_space=pltpu.VMEM)
    params = pltpu.CompilerParams(vmem_limit_bytes=24 << 20)
    width = own_pad + share

    def swap_row(x, bits):
        return lax.ppermute(x, "row", [(i, i ^ bits) for i in range(n_row)])

    def swap_col(x):
        return lax.ppermute(x, "col", [(0, 1), (1, 0)])

    relative = n_row == 8
    matrix = pl.pallas_call(
        functools.partial(matrix_kernel, relative),
        out_shape=jax.ShapeDtypeStruct((kept, frames), jnp.float32),
        in_specs=[smem, smem, smem],
        out_specs=vmem,
        cost_estimate=pl.CostEstimate(flops=10**10, transcendentals=0, bytes_accessed=10**8),
        compiler_params=params,
    )(tap_values, tap_count, kept_frames)
    if relative:
        slabs = jax.ShapeDtypeStruct((n_row, 8, width), jnp.float32)
        straight, cross = pl.pallas_call(
            functools.partial(pack_kernel, own),
            out_shape=(slabs, slabs),
            in_specs=[vmem, vmem],
            out_specs=(vmem, vmem),
            scratch_shapes=[pltpu.VMEM((8, B), jnp.float32)],
            compiler_params=params,
        )(band_start.reshape(1, 1), series)
        one, two = (jax.ShapeDtypeStruct((16 * count, width), jnp.float32) for count in (1, 2))
        own_raw, y_raw, z_raw, *far_raws = pl.pallas_call(
            merge_kernel,
            out_shape=[one, two, two] + [one] * (n_row - 4),
            in_specs=[vmem, vmem, smem],
            out_specs=[vmem] * (n_row - 1),
            compiler_params=params,
        )(straight, swap_col(cross), tap_count)
        raws = [swap_row(raw, mask) for mask, raw in enumerate(far_raws, 4)]
        z_raw = swap_row(z_raw, 2)
        y_raw = pl.pallas_call(
            relay_kernel,
            out_shape=two,
            in_specs=[vmem, vmem],
            out_specs=vmem,
            input_output_aliases={0: 0},
            compiler_params=params,
        )(y_raw, z_raw)
        raws += [swap_row(y_raw, 1), z_raw, own_raw]
    else:
        packed = pl.pallas_call(
            functools.partial(pack_all_kernel, own),
            out_shape=jax.ShapeDtypeStruct((n_dev, 8, width), jnp.float32),
            in_specs=[vmem, vmem],
            out_specs=vmem,
            scratch_shapes=[pltpu.VMEM((8, B), jnp.float32)],
            compiler_params=params,
        )(band_start.reshape(1, 1), series)
        raws = [lax.all_to_all(packed, AXES, 0, 0, tiled=True).reshape(frames, width)]
    block = pl.pallas_call(
        functools.partial(scale_band_kernel, own_pad),
        out_shape=jax.ShapeDtypeStruct((kept, share), jnp.bfloat16),
        in_specs=[vmem] * (1 + len(raws)),
        out_specs=vmem,
        compiler_params=params,
    )(matrix, *raws)
    own_rows = pl.pallas_call(
        functools.partial(scale_own_kernel, own_pad),
        out_shape=jax.ShapeDtypeStruct((own, kept), jnp.bfloat16),
        in_specs=[vmem] * (1 + len(raws)),
        out_specs=vmem,
        compiler_params=params,
    )(matrix, *raws)

    across = swap_row(block, 3)
    near = swap_row(block, 2)
    side = swap_row(block, 1)
    out = fisher_part(own_rows, [(0, block), (4, swap_col(block))], None)
    across, out = lax.optimization_barrier((across, out))
    out = fisher_part(own_rows, [(1, side), (2, near), (3, across)], out)
    late = [(5, swap_col(side)), (6, swap_col(near)), (7, swap_col(across))]
    out = fisher_part(own_rows, late, out)
    return out.T


def solution(mesh):
    placed = (P(("subj", "row", "col"), None), P(), P(), P("subj"), P("subj"))
    return jax.shard_map(
        body, mesh=mesh, in_specs=placed, out_specs=P("subj", ("row", "col")), check_vma=False
    )
```

```python
import functools

import jax
import jax.numpy as jnp
from jax import lax
from jax.experimental import pallas as pl
from jax.experimental.pallas import tpu as pltpu
from jax.sharding import PartitionSpec as P

B = 4096
LANES = 128
EPSILON = 1e-06
CLIP_LIMIT = 0.999
HALF_LN2 = 0.34657359027997264
GROUP = 8
AXES = ("row", "col")


def round_up(value, unit):
    return (value + unit - 1) // unit * unit


def band_place(device):
    row, col = device // 2, device % 2
    return col * 4 + row % 4


def shift_band(start_ref, series_ref, band_ref):
    total = series_ref.shape[1]
    start = jnp.max(start_ref[...])
    base = pl.multiple_of(jnp.minimum(start // LANES * LANES, total - B - LANES), LANES)
    rest = start - base
    shift = lax.rem(LANES - rest, LANES)
    lane = lax.broadcasted_iota(jnp.int32, (8, LANES), 1)
    here = lane < LANES - rest
    before = pltpu.roll(series_ref[:, pl.ds(base, LANES)], shift, 1)
    for tile in range(B // LANES):
        after = pltpu.roll(series_ref[:, pl.ds(base + (tile + 1) * LANES, LANES)], shift, 1)
        band_ref[:, tile * LANES : (tile + 1) * LANES] = jnp.where(here, before, after)
        before = after


def own_columns(device, own, own_pad, series_ref):
    columns = series_ref[:, device * own : (device + 1) * own]
    if own_pad > own:
        columns = jnp.concatenate([columns, jnp.zeros((8, own_pad - own), jnp.float32)], 1)
    return columns


def pack_all_kernel(own, start_ref, series_ref, out_ref, band_ref):
    share = B // GROUP
    own_pad = out_ref.shape[2] - share
    shift_band(start_ref, series_ref, band_ref)
    for device in range(out_ref.shape[0]):
        out_ref[device, :, :own_pad] = own_columns(device, own, own_pad, series_ref)
        place = band_place(device)
        out_ref[device, :, own_pad:] = band_ref[:, place * share : (place + 1) * share]


def pack_kernel(own, start_ref, series_ref, straight_ref, cross_ref, band_ref):
    share = B // GROUP
    own_pad = straight_ref.shape[2] - share
    first_core = lax.axis_index("col") == 0
    shift_band(start_ref, series_ref, band_ref)
    for row in range(straight_ref.shape[0]):
        slabs = []
        for device in (2 * row, 2 * row + 1):
            place = band_place(device)
            slabs.append(
                (
                    own_columns(device, own, own_pad, series_ref),
                    band_ref[:, place * share : (place + 1) * share],
                )
            )
        for (low, high), zero, one in zip(((0, own_pad), (own_pad, own_pad + share)), *slabs):
            straight_ref[row, :, low:high] = jnp.where(first_core, zero, one)
            cross_ref[row, :, low:high] = jnp.where(first_core, one, zero)


def merge_kernel(straight_ref, crossed_ref, _, own_ref, y_ref, z_ref, *far_refs):
    row = lax.axis_index("row")
    spots = [(own_ref, 0), (y_ref, 0), (z_ref, 0), (z_ref, 16), *((ref, 0) for ref in far_refs)]
    for mask, (out_ref, at) in enumerate(spots):
        out_ref[at : at + 8] = straight_ref[row ^ mask]
        out_ref[at + 8 : at + 16] = crossed_ref[row ^ mask]


def relay_kernel(y_ref, z_ref, out_ref):
    out_ref[:16] = y_ref[:16]
    out_ref[16:] = z_ref[16:]


def frames_of(refs, low, high):
    if len(refs) == 1:
        return refs[0][:, low:high]
    *far_refs, y_ref, z_ref, own_ref = refs
    near = [own_ref[...], y_ref[:16], z_ref[:16], y_ref[16:]]
    return jnp.concatenate([part[:, low:high] for part in near + [ref[...] for ref in far_refs]], 0)


def filter_matrix(kept, frames, turn, taps_ref, count_ref, kept_ref):
    n_taps = taps_ref.shape[0]
    reach = n_taps // 2
    shape = (kept, LANES)
    place = lax.broadcasted_iota(jnp.int32, shape, 0)

    def skip(block, carry):
        frame, seen = carry
        seen = seen + kept_ref[block]
        return frame + jnp.where(place >= seen, 8 - kept_ref[block], 0), seen

    frame, _ = lax.fori_loop(0, frames // 8, skip, (place, jnp.int32(0)), unroll=frames <= 128)
    reach_used = count_ref[0]
    tap_sum = jnp.float32(0)
    tap_number = jnp.float32(0)
    for tap in range(n_taps):
        used = abs(tap - reach) <= reach_used
        tap_sum = tap_sum + jnp.where(used, taps_ref[tap], 0.0)
        tap_number = tap_number + jnp.where(used, 1.0, 0.0)
    centre = jnp.full(shape, tap_sum, jnp.float32) / jnp.full(shape, tap_number, jnp.float32)
    pieces = []
    for tile in range(frames // LANES):
        offset = ((lax.broadcasted_iota(jnp.int32, shape, 1) + tile * LANES) ^ turn) - frame
        value = jnp.zeros(shape, jnp.float32)
        for tap in range(n_taps):
            value = jnp.where(offset == tap - reach, taps_ref[tap], value)
        pieces.append(jnp.where(jnp.abs(offset) <= reach_used, value - centre, 0.0))
    return pieces[0] if len(pieces) == 1 else jnp.concatenate(pieces, 1)


def matrix_kernel(relative, taps_ref, count_ref, kept_ref, out_ref):
    kept, frames = out_ref.shape
    turn = 8 * (2 * lax.axis_index("row") + lax.axis_index("col")) if relative else 0
    out_ref[...] = filter_matrix(kept, frames, turn, taps_ref, count_ref, kept_ref)


def scaled_columns(matrix, raw):
    centered = jnp.dot(
        matrix, raw, precision=lax.Precision.HIGHEST, preferred_element_type=jnp.float32
    )
    spread = jnp.sum(centered * centered, axis=0, keepdims=True)
    return centered * lax.rsqrt(spread + EPSILON)


def scale_band_kernel(first, matrix_ref, *refs):
    *raw_refs, band_ref = refs
    raw = frames_of(raw_refs, first, first + band_ref.shape[1])
    band_ref[...] = scaled_columns(matrix_ref[...], raw).astype(jnp.bfloat16)


def scale_own_kernel(end, matrix_ref, *refs):
    *raw_refs, own_ref = refs
    raw = frames_of(raw_refs, 0, end)
    scaled = scaled_columns(matrix_ref[...], raw)
    own_ref[...] = scaled.T[: own_ref.shape[0]].astype(jnp.bfloat16)


def fisher_kernel(flips, own_ref, *refs):
    pieces = refs[: len(flips)]
    out_ref, made_ref, sems = refs[-3:]
    share = pieces[0].shape[1]
    half = share // 2
    place = lax.axis_index("col") * 4 + lax.axis_index("row") % 4
    copies = []
    for at, (flip, piece_ref) in enumerate(zip(flips, pieces)):
        for low in (0, half):
            correlation = jnp.dot(
                own_ref[...], piece_ref[:, low : low + half], preferred_element_type=jnp.float32
            )
            c = jnp.clip(correlation, -CLIP_LIMIT, CLIP_LIMIT)
            z_value = HALF_LN2 * (jnp.log2(1.0 + c) - jnp.log2(1.0 - c))
            made_ref[:, at * share + low : at * share + low + half] = z_value.astype(jnp.bfloat16)
        where = pl.multiple_of((place ^ flip) * share, share)
        copy = pltpu.make_async_copy(
            made_ref.at[:, at * share : (at + 1) * share],
            out_ref.at[:, pl.ds(where, share)],
            sems.at[at],
        )
        copy.start()
        copies.append(copy)
    for copy in copies:
        copy.wait()


def first_kernel(end, flips, count, matrix_ref, *refs):
    raw_refs, pieces = refs[:count], refs[count : count + len(flips)]
    out_ref, own_ref, made_ref, sems = refs[count + len(flips) :]
    scale_own_kernel(end, matrix_ref, *raw_refs, own_ref)
    fisher_kernel(flips, own_ref, *pieces, out_ref, made_ref, sems)


def fisher_part(own_rows, pieces, out):
    flips = [flip for flip, _ in pieces]
    arrays = [array for _, array in pieces]
    own = own_rows.shape[0]
    vmem = pl.BlockSpec(memory_space=pltpu.VMEM)
    specs = [vmem] * (1 + len(arrays))
    args = [own_rows, *arrays]
    aliases = {}
    if out is not None:
        specs.append(pl.BlockSpec(memory_space=pltpu.HBM))
        aliases = {len(args): 0}
        args.append(out)
    return pl.pallas_call(
        functools.partial(fisher_kernel, flips),
        out_shape=jax.ShapeDtypeStruct((own, B), jnp.bfloat16),
        in_specs=specs,
        out_specs=pl.BlockSpec(memory_space=pltpu.HBM),
        scratch_shapes=[
            pltpu.VMEM((own, len(arrays) * arrays[0].shape[1]), jnp.bfloat16),
            pltpu.SemaphoreType.DMA((len(arrays),)),
        ],
        input_output_aliases=aliases,
        compiler_params=pltpu.CompilerParams(vmem_limit_bytes=48 << 20),
    )(*args)


def body(series, tap_values, tap_count, kept_frames, band_start):
    n_row = lax.axis_size("row")
    n_dev = n_row * lax.axis_size("col")
    frames = 8 * n_dev
    kept = frames * 3 // 4
    total = series.shape[1]
    own = total // n_dev
    own_pad = round_up(own, LANES)
    share = B // GROUP
    smem = pl.BlockSpec(memory_space=pltpu.SMEM)
    vmem = pl.BlockSpec(memory_space=pltpu.VMEM)
    params = pltpu.CompilerParams(vmem_limit_bytes=24 << 20)
    width = own_pad + share

    def swap_row(x, bits):
        return lax.ppermute(x, "row", [(i, i ^ bits) for i in range(n_row)])

    def swap_col(x):
        return lax.ppermute(x, "col", [(0, 1), (1, 0)])

    relative = n_row == 8
    matrix = pl.pallas_call(
        functools.partial(matrix_kernel, relative),
        out_shape=jax.ShapeDtypeStruct((kept, frames), jnp.float32),
        in_specs=[smem, smem, smem],
        out_specs=vmem,
        cost_estimate=pl.CostEstimate(flops=10**10, transcendentals=0, bytes_accessed=10**8),
        compiler_params=params,
    )(tap_values, tap_count, kept_frames)
    if relative:
        slabs = jax.ShapeDtypeStruct((n_row, 8, width), jnp.float32)
        straight, cross = pl.pallas_call(
            functools.partial(pack_kernel, own),
            out_shape=(slabs, slabs),
            in_specs=[vmem, vmem],
            out_specs=(vmem, vmem),
            scratch_shapes=[pltpu.VMEM((8, B), jnp.float32)],
            compiler_params=params,
        )(band_start.reshape(1, 1), series)
        one, two = (jax.ShapeDtypeStruct((16 * count, width), jnp.float32) for count in (1, 2))
        own_raw, y_raw, z_raw, *far_raws = pl.pallas_call(
            merge_kernel,
            out_shape=[one, two, two] + [one] * (n_row - 4),
            in_specs=[vmem, vmem, smem],
            out_specs=[vmem] * (n_row - 1),
            compiler_params=params,
        )(straight, swap_col(cross), tap_count)
        raws = [swap_row(raw, mask) for mask, raw in enumerate(far_raws, 4)]
        z_raw = swap_row(z_raw, 2)
        y_raw = pl.pallas_call(
            relay_kernel,
            out_shape=two,
            in_specs=[vmem, vmem],
            out_specs=vmem,
            input_output_aliases={0: 0},
            compiler_params=params,
        )(y_raw, z_raw)
        raws += [swap_row(y_raw, 1), z_raw, own_raw]
    else:
        packed = pl.pallas_call(
            functools.partial(pack_all_kernel, own),
            out_shape=jax.ShapeDtypeStruct((n_dev, 8, width), jnp.float32),
            in_specs=[vmem, vmem],
            out_specs=vmem,
            scratch_shapes=[pltpu.VMEM((8, B), jnp.float32)],
            compiler_params=params,
        )(band_start.reshape(1, 1), series)
        raws = [lax.all_to_all(packed, AXES, 0, 0, tiled=True).reshape(frames, width)]
    block = pl.pallas_call(
        functools.partial(scale_band_kernel, own_pad),
        out_shape=jax.ShapeDtypeStruct((kept, share), jnp.bfloat16),
        in_specs=[vmem] * (1 + len(raws)),
        out_specs=vmem,
        compiler_params=params,
    )(matrix, *raws)
    across = swap_row(block, 3)
    near = swap_row(block, 2)
    side = swap_row(block, 1)
    out, own_rows = pl.pallas_call(
        functools.partial(first_kernel, own_pad, (0, 4), len(raws)),
        out_shape=(
            jax.ShapeDtypeStruct((own, B), jnp.bfloat16),
            jax.ShapeDtypeStruct((own, kept), jnp.bfloat16),
        ),
        in_specs=[vmem] * (3 + len(raws)),
        out_specs=(pl.BlockSpec(memory_space=pltpu.HBM), vmem),
        scratch_shapes=[
            pltpu.VMEM((own, 2 * share), jnp.bfloat16),
            pltpu.SemaphoreType.DMA((2,)),
        ],
        compiler_params=pltpu.CompilerParams(vmem_limit_bytes=48 << 20),
    )(matrix, *raws, block, swap_col(block))
    across, out = lax.optimization_barrier((across, out))
    out = fisher_part(own_rows, [(1, side), (2, near), (3, across)], out)
    late = [(5, swap_col(side)), (6, swap_col(near)), (7, swap_col(across))]
    out = fisher_part(own_rows, late, out)
    return out.T


def solution(mesh):
    placed = (P(("subj", "row", "col"), None), P(), P(), P("subj"), P("subj"))
    return jax.shard_map(
        body, mesh=mesh, in_specs=placed, out_specs=P("subj", ("row", "col")), check_vma=False
    )
```

```python
import functools

import jax
import jax.numpy as jnp
from jax import lax
from jax.experimental import pallas as pl
from jax.experimental.pallas import tpu as pltpu
from jax.sharding import PartitionSpec as P

B = 4096
LANES = 128
EPSILON = 1e-06
CLIP_LIMIT = 0.999
HALF_LN2 = 0.34657359027997264
GROUP = 8
AXES = ("row", "col")


def round_up(value, unit):
    return (value + unit - 1) // unit * unit


def band_place(device):
    row, col = device // 2, device % 2
    return col * 4 + row % 4


def shift_band(start_ref, series_ref, band_ref):
    total = series_ref.shape[1]
    start = jnp.max(start_ref[...])
    base = pl.multiple_of(jnp.minimum(start // LANES * LANES, total - B - LANES), LANES)
    rest = start - base
    shift = lax.rem(LANES - rest, LANES)
    lane = lax.broadcasted_iota(jnp.int32, (8, LANES), 1)
    here = lane < LANES - rest
    before = pltpu.roll(series_ref[:, pl.ds(base, LANES)], shift, 1)
    for tile in range(B // LANES):
        after = pltpu.roll(series_ref[:, pl.ds(base + (tile + 1) * LANES, LANES)], shift, 1)
        band_ref[:, tile * LANES : (tile + 1) * LANES] = jnp.where(here, before, after)
        before = after


def own_columns(device, own, own_pad, series_ref):
    columns = series_ref[:, device * own : (device + 1) * own]
    if own_pad > own:
        columns = jnp.concatenate([columns, jnp.zeros((8, own_pad - own), jnp.float32)], 1)
    return columns


def pack_all_kernel(own, start_ref, series_ref, out_ref, band_ref):
    share = B // GROUP
    own_pad = out_ref.shape[2] - share
    shift_band(start_ref, series_ref, band_ref)
    for device in range(out_ref.shape[0]):
        out_ref[device, :, :own_pad] = own_columns(device, own, own_pad, series_ref)
        place = band_place(device)
        out_ref[device, :, own_pad:] = band_ref[:, place * share : (place + 1) * share]


def pack_kernel(own, start_ref, series_ref, straight_ref, cross_ref, band_ref):
    share = B // GROUP
    own_pad = straight_ref.shape[2] - share
    first_core = lax.axis_index("col") == 0
    shift_band(start_ref, series_ref, band_ref)
    for row in range(straight_ref.shape[0]):
        slabs = []
        for device in (2 * row, 2 * row + 1):
            place = band_place(device)
            slabs.append(
                (
                    own_columns(device, own, own_pad, series_ref),
                    band_ref[:, place * share : (place + 1) * share],
                )
            )
        for (low, high), zero, one in zip(((0, own_pad), (own_pad, own_pad + share)), *slabs):
            straight_ref[row, :, low:high] = jnp.where(first_core, zero, one)
            cross_ref[row, :, low:high] = jnp.where(first_core, one, zero)


def merge_kernel(straight_ref, crossed_ref, _, own_ref, y_ref, z_ref, *far_refs):
    row = lax.axis_index("row")
    spots = [(own_ref, 0), (y_ref, 0), (z_ref, 0), (z_ref, 16), *((ref, 0) for ref in far_refs)]
    for mask, (out_ref, at) in enumerate(spots):
        out_ref[at : at + 8] = straight_ref[row ^ mask]
        out_ref[at + 8 : at + 16] = crossed_ref[row ^ mask]


def relay_kernel(y_ref, z_ref, out_ref):
    out_ref[:16] = y_ref[:16]
    out_ref[16:] = z_ref[16:]


def frames_of(refs, low, high):
    if len(refs) == 1:
        return refs[0][:, low:high]
    *far_refs, y_ref, z_ref, own_ref = refs
    near = [own_ref[...], y_ref[:16], z_ref[:16], y_ref[16:]]
    return jnp.concatenate([part[:, low:high] for part in near + [ref[...] for ref in far_refs]], 0)


def filter_matrix(kept, frames, turn, taps_ref, count_ref, kept_ref):
    n_taps = taps_ref.shape[0]
    reach = n_taps // 2
    shape = (kept, LANES)
    place = lax.broadcasted_iota(jnp.int32, shape, 0)

    def skip(block, carry):
        frame, seen = carry
        seen = seen + kept_ref[block]
        return frame + jnp.where(place >= seen, 8 - kept_ref[block], 0), seen

    frame, _ = lax.fori_loop(0, frames // 8, skip, (place, jnp.int32(0)), unroll=frames <= 128)
    reach_used = count_ref[0]
    tap_sum = jnp.float32(0)
    tap_number = jnp.float32(0)
    for tap in range(n_taps):
        used = abs(tap - reach) <= reach_used
        tap_sum = tap_sum + jnp.where(used, taps_ref[tap], 0.0)
        tap_number = tap_number + jnp.where(used, 1.0, 0.0)
    centre = jnp.full(shape, tap_sum, jnp.float32) / jnp.full(shape, tap_number, jnp.float32)
    pieces = []
    for tile in range(frames // LANES):
        offset = ((lax.broadcasted_iota(jnp.int32, shape, 1) + tile * LANES) ^ turn) - frame
        value = jnp.zeros(shape, jnp.float32)
        for tap in range(n_taps):
            value = jnp.where(offset == tap - reach, taps_ref[tap], value)
        pieces.append(jnp.where(jnp.abs(offset) <= reach_used, value - centre, 0.0))
    return pieces[0] if len(pieces) == 1 else jnp.concatenate(pieces, 1)


def matrix_kernel(relative, taps_ref, count_ref, kept_ref, out_ref):
    kept, frames = out_ref.shape
    turn = 8 * (2 * lax.axis_index("row") + lax.axis_index("col")) if relative else 0
    out_ref[...] = filter_matrix(kept, frames, turn, taps_ref, count_ref, kept_ref)


def scaled_columns(matrix, raw):
    centered = jnp.dot(
        matrix, raw, precision=lax.Precision.HIGHEST, preferred_element_type=jnp.float32
    )
    spread = jnp.sum(centered * centered, axis=0, keepdims=True)
    return centered * lax.rsqrt(spread + EPSILON)


def scale_band_kernel(first, matrix_ref, *refs):
    *raw_refs, band_ref = refs
    raw = frames_of(raw_refs, first, first + band_ref.shape[1])
    band_ref[...] = scaled_columns(matrix_ref[...], raw).astype(jnp.bfloat16)


def scale_own_kernel(end, matrix_ref, *refs):
    *raw_refs, own_ref = refs
    raw = frames_of(raw_refs, 0, end)
    scaled = scaled_columns(matrix_ref[...], raw)
    own_ref[...] = scaled.T[: own_ref.shape[0]].astype(jnp.bfloat16)


def fisher_kernel(flips, own_ref, *refs):
    pieces = refs[: len(flips)]
    out_ref, made_ref, sems = refs[-3:]
    share = pieces[0].shape[1]
    half = share // 2
    place = lax.axis_index("col") * 4 + lax.axis_index("row") % 4
    copies = []
    for at, (flip, piece_ref) in enumerate(zip(flips, pieces)):
        for low in (0, half):
            correlation = jnp.dot(
                own_ref[...], piece_ref[:, low : low + half], preferred_element_type=jnp.float32
            )
            c = jnp.clip(correlation, -CLIP_LIMIT, CLIP_LIMIT)
            z_value = HALF_LN2 * (jnp.log2(1.0 + c) - jnp.log2(1.0 - c))
            made_ref[:, at * share + low : at * share + low + half] = z_value.astype(jnp.bfloat16)
            where = pl.multiple_of((place ^ flip) * share + low, half)
            copy = pltpu.make_async_copy(
                made_ref.at[:, at * share + low : at * share + low + half],
                out_ref.at[:, pl.ds(where, half)],
                sems.at[len(copies)],
            )
            copy.start()
            copies.append(copy)
    for copy in copies:
        copy.wait()


def first_kernel(end, flips, count, matrix_ref, *refs):
    raw_refs, pieces = refs[:count], refs[count : count + len(flips)]
    out_ref, own_ref, made_ref, sems = refs[count + len(flips) :]
    scale_own_kernel(end, matrix_ref, *raw_refs, own_ref)
    fisher_kernel(flips, own_ref, *pieces, out_ref, made_ref, sems)


def fisher_part(own_rows, pieces, out):
    flips = [flip for flip, _ in pieces]
    arrays = [array for _, array in pieces]
    own = own_rows.shape[0]
    vmem = pl.BlockSpec(memory_space=pltpu.VMEM)
    specs = [vmem] * (1 + len(arrays))
    args = [own_rows, *arrays]
    aliases = {}
    if out is not None:
        specs.append(pl.BlockSpec(memory_space=pltpu.HBM))
        aliases = {len(args): 0}
        args.append(out)
    return pl.pallas_call(
        functools.partial(fisher_kernel, flips),
        out_shape=jax.ShapeDtypeStruct((own, B), jnp.bfloat16),
        in_specs=specs,
        out_specs=pl.BlockSpec(memory_space=pltpu.HBM),
        scratch_shapes=[
            pltpu.VMEM((own, len(arrays) * arrays[0].shape[1]), jnp.bfloat16),
            pltpu.SemaphoreType.DMA((2 * len(arrays),)),
        ],
        input_output_aliases=aliases,
        compiler_params=pltpu.CompilerParams(vmem_limit_bytes=48 << 20),
    )(*args)


def body(series, tap_values, tap_count, kept_frames, band_start):
    n_row = lax.axis_size("row")
    n_dev = n_row * lax.axis_size("col")
    frames = 8 * n_dev
    kept = frames * 3 // 4
    total = series.shape[1]
    own = total // n_dev
    own_pad = round_up(own, LANES)
    share = B // GROUP
    smem = pl.BlockSpec(memory_space=pltpu.SMEM)
    vmem = pl.BlockSpec(memory_space=pltpu.VMEM)
    params = pltpu.CompilerParams(vmem_limit_bytes=24 << 20)
    width = own_pad + share

    def swap_row(x, bits):
        return lax.ppermute(x, "row", [(i, i ^ bits) for i in range(n_row)])

    def swap_col(x):
        return lax.ppermute(x, "col", [(0, 1), (1, 0)])

    relative = n_row == 8
    matrix = pl.pallas_call(
        functools.partial(matrix_kernel, relative),
        out_shape=jax.ShapeDtypeStruct((kept, frames), jnp.float32),
        in_specs=[smem, smem, smem],
        out_specs=vmem,
        cost_estimate=pl.CostEstimate(flops=10**10, transcendentals=0, bytes_accessed=10**8),
        compiler_params=params,
    )(tap_values, tap_count, kept_frames)
    if relative:
        slabs = jax.ShapeDtypeStruct((n_row, 8, width), jnp.float32)
        straight, cross = pl.pallas_call(
            functools.partial(pack_kernel, own),
            out_shape=(slabs, slabs),
            in_specs=[vmem, vmem],
            out_specs=(vmem, vmem),
            scratch_shapes=[pltpu.VMEM((8, B), jnp.float32)],
            compiler_params=params,
        )(band_start.reshape(1, 1), series)
        one, two = (jax.ShapeDtypeStruct((16 * count, width), jnp.float32) for count in (1, 2))
        own_raw, y_raw, z_raw, *far_raws = pl.pallas_call(
            merge_kernel,
            out_shape=[one, two, two] + [one] * (n_row - 4),
            in_specs=[vmem, vmem, smem],
            out_specs=[vmem] * (n_row - 1),
            compiler_params=params,
        )(straight, swap_col(cross), tap_count)
        raws = [swap_row(raw, mask) for mask, raw in enumerate(far_raws, 4)]
        z_raw = swap_row(z_raw, 2)
        y_raw = pl.pallas_call(
            relay_kernel,
            out_shape=two,
            in_specs=[vmem, vmem],
            out_specs=vmem,
            input_output_aliases={0: 0},
            compiler_params=params,
        )(y_raw, z_raw)
        raws += [swap_row(y_raw, 1), z_raw, own_raw]
    else:
        packed = pl.pallas_call(
            functools.partial(pack_all_kernel, own),
            out_shape=jax.ShapeDtypeStruct((n_dev, 8, width), jnp.float32),
            in_specs=[vmem, vmem],
            out_specs=vmem,
            scratch_shapes=[pltpu.VMEM((8, B), jnp.float32)],
            compiler_params=params,
        )(band_start.reshape(1, 1), series)
        raws = [lax.all_to_all(packed, AXES, 0, 0, tiled=True).reshape(frames, width)]
    block = pl.pallas_call(
        functools.partial(scale_band_kernel, own_pad),
        out_shape=jax.ShapeDtypeStruct((kept, share), jnp.bfloat16),
        in_specs=[vmem] * (1 + len(raws)),
        out_specs=vmem,
        compiler_params=params,
    )(matrix, *raws)
    across = swap_row(block, 3)
    near = swap_row(block, 2)
    side = swap_row(block, 1)
    out, own_rows = pl.pallas_call(
        functools.partial(first_kernel, own_pad, (0, 4), len(raws)),
        out_shape=(
            jax.ShapeDtypeStruct((own, B), jnp.bfloat16),
            jax.ShapeDtypeStruct((own, kept), jnp.bfloat16),
        ),
        in_specs=[vmem] * (3 + len(raws)),
        out_specs=(pl.BlockSpec(memory_space=pltpu.HBM), vmem),
        scratch_shapes=[
            pltpu.VMEM((own, 2 * share), jnp.bfloat16),
            pltpu.SemaphoreType.DMA((4,)),
        ],
        compiler_params=pltpu.CompilerParams(vmem_limit_bytes=48 << 20),
    )(matrix, *raws, block, swap_col(block))
    across, out = lax.optimization_barrier((across, out))
    out = fisher_part(own_rows, [(1, side), (2, near), (3, across)], out)
    late = [(5, swap_col(side)), (6, swap_col(near)), (7, swap_col(across))]
    out = fisher_part(own_rows, late, out)
    return out.T


def solution(mesh):
    placed = (P(("subj", "row", "col"), None), P(), P(), P("subj"), P("subj"))
    return jax.shard_map(
        body, mesh=mesh, in_specs=placed, out_specs=P("subj", ("row", "col")), check_vma=False
    )
```
